32 devices in a mesh: groups: 2 (over x), seq: 16 (over z, y, core).
Axes of the slice: x: 2, y: 2, z: 4, core: 2. Of those that a mesh axis runs over, the one named last changes fastest.
Arguments:
- self_query: bfloat16 [4096, 5120], P(('groups', 'seq')), parts along dimension 0, may hold values from -384 to 384
- self_key: bfloat16 [4096, 5120], P(('groups', 'seq')), parts along dimension 0, may hold values from -20 to 20
- self_value: bfloat16 [4096, 5120], P(('groups', 'seq')), parts along dimension 0, may hold values from -6 to 6
- cross_query: bfloat16 [4096, 5120], P(('groups', 'seq')), parts along dimension 0, may hold values from -384 to 384
- context: bfloat16 [512, 4096], P('groups'), parts along dimension 0, may hold values from -6 to 6
- key_weight: bfloat16 [4096, 5120], P(None, 'seq'), may hold values from -0.09375 to 0.09375
- value_weight: bfloat16 [4096, 5120], P(None, 'seq'), may hold values from -0.09375 to 0.09375
- band_width: int32 [40], replicated, may hold values from 0 to 15
Outputs:
- self_out: bfloat16 [4096, 5120], P(('groups', 'seq')), parts along dimension 0
- cross_out: bfloat16 [4096, 5120], P(('groups', 'seq')), parts along dimension 0
The draws below stay inside these ranges and needn't reach their ends.
There are 2 independent parts, one for each index of `groups`. The reference program is written for one: setup_inputs(seed, part) draws one part's arguments, and reference() takes and returns one part's arrays. A program takes and returns all parts, laid end to end along the dimension named above; an argument that names none is the same for every part. Nothing has to cross between parts.
All inputs are finite; a program needn't handle non-finite values.
Results may differ from the reference program's by a relative error of at most 0.006.
The reference program's roundings to bfloat16 on the way count: a program that leaves them out, or rounds other values in their place, can miss the bound.
Values may be sent and summed in bfloat16 or wider, within the bound.
No kernel may reach another device: no remote copies, remote signals or barrier semaphores. Data moves between devices by JAX's collectives and lax.ppermute only.
A program may use at most 128 MiB of HBM per device.

```python
import math
import jax
import jax.numpy as jnp
from jax import lax

H = 40
HD = 128
CTX = 4096
D = 5120
TXT = 256
TOK_DEV = 128
SB = 16
TOKENS = 2048


def scaled_rows(key, row_count, col_count):
    noise_key = jax.random.fold_in(key, 0)
    values = jnp.clip(jax.random.normal(noise_key, (row_count, col_count), jnp.float32), -4.0, 4.0)
    return values


def draw_self_query(key, part):
    return scaled_rows(jax.random.fold_in(key, 11), TOKENS, D).astype(jnp.bfloat16)


def draw_self_key(key, part):
    return scaled_rows(jax.random.fold_in(key, 12), TOKENS, D).astype(jnp.bfloat16)


def draw_cross_query(key, part):
    return scaled_rows(jax.random.fold_in(key, 13), TOKENS, D).astype(jnp.bfloat16)


def touch_ends(entries, own_key, low, top_value):
    extent = entries.shape
    index_at = [jax.random.randint(jax.random.fold_in(own_key, axis), (), 0, extent[axis]) for axis in range(len(extent))]
    entries = entries.at[tuple(index_at)].set(low)
    longest = extent.index(max(extent))
    index_at[longest] = (index_at[longest] + 1) % extent[longest]
    return entries.at[tuple(index_at)].set(top_value)


def steps_of(rng, shape, pieces, low, high):
    loudness = 1.0
    for dim, shards_of in pieces:
        steps = jax.random.uniform(jax.random.fold_in(jax.random.fold_in(rng, 6), dim), (shards_of,), jnp.float32, low / len(pieces), high / len(pieces))
        loudness = loudness * jnp.repeat(jnp.exp(steps), shape[dim] // shards_of).reshape((-1,) + (1,) * (len(shape) - 1 - dim))
    return loudness


def normal_values(key, extent, scale, most, shards=(), kind=jnp.bfloat16):
    level = steps_of(key, extent, shards, -0.22, 0.18) if shards else 1.0
    entries = jax.random.normal(key, extent, jnp.float32) * scale * level
    return jnp.minimum(jnp.maximum(entries, -most), most).astype(kind)


def setup_inputs(seed: int = 0, part: int = 0) -> dict:
    key_list = jax.random.split(jax.random.key(seed), 9)
    part_splits = jax.random.split(jax.random.fold_in(key_list[8], part), 9)
    return {
        "self_query": draw_self_query(jax.random.fold_in(jax.random.fold_in(key_list[8], part), 71), part),
        "self_key": draw_self_key(jax.random.fold_in(jax.random.fold_in(key_list[8], part), 71), part),
        "self_value": normal_values(part_splits[2], (TOKENS, D), 1.0, 6.0, ((0, 16),)),
        "cross_query": draw_cross_query(jax.random.fold_in(jax.random.fold_in(key_list[8], part), 71), part),
        "context": normal_values(part_splits[4], (TXT, CTX), 1.0, 6.0),
        "key_weight": normal_values(key_list[5], (CTX, D), CTX ** -0.5, 0.09375, ((1, 16),)),
        "value_weight": normal_values(key_list[6], (CTX, D), CTX ** -0.5, 0.09375, ((1, 16),)),
        "band_width": touch_ends(jax.random.randint(key_list[7], (H,), 0, SB), jax.random.fold_in(key_list[7], 1), 0, SB - 1).astype(jnp.int32),
    }


def reference(self_query, self_key, self_value, cross_query, context, key_weight, value_weight, band_width):
    softmax_scale = 1.0 / math.sqrt(HD)
    stripe_len = SB * TOK_DEV
    stripe_count = TOKENS // stripe_len

    def heads_major(source):
        return source.reshape(stripe_count, stripe_len, H, HD).transpose(2, 0, 1, 3)
    block_ids = jnp.arange(stripe_len, dtype=jnp.int32) // TOK_DEV
    block_gap = jnp.abs(block_ids[:, None] - block_ids[None, :])

    def self_head(inputs):
        head_query, head_key, head_value, head_band = inputs
        scores = jnp.einsum('nqd,nkd->nqk', head_query.astype(jnp.float32), head_key.astype(jnp.float32)) * softmax_scale
        allowed = (block_gap <= head_band)[None]
        scores = jnp.where(allowed, scores, -jnp.inf)
        row_max = lax.optimization_barrier(jnp.max(scores, axis=-1, keepdims=True))
        weights = jnp.exp(scores - row_max)
        row_sum = lax.optimization_barrier(jnp.sum(weights, axis=-1, keepdims=True))
        attended = jnp.einsum('nqk,nkd->nqd', weights.astype(jnp.bfloat16).astype(jnp.float32), head_value.astype(jnp.float32))
        return (attended / row_sum).astype(jnp.bfloat16)
    self_heads = lax.map(self_head, (heads_major(self_query), heads_major(self_key), heads_major(self_value), band_width))
    self_out = self_heads.transpose(1, 2, 0, 3).reshape(TOKENS, H * HD)
    text_key = jnp.dot(context, key_weight, preferred_element_type=jnp.float32).astype(jnp.bfloat16)
    text_value = jnp.dot(context, value_weight, preferred_element_type=jnp.float32).astype(jnp.bfloat16)
    text_keys = text_key.reshape(TXT, H, HD).transpose(1, 0, 2)
    text_values = text_value.reshape(TXT, H, HD).transpose(1, 0, 2)
    cross_heads_in = cross_query.reshape(TOKENS, H, HD).transpose(1, 0, 2)

    def cross_head(inputs):
        head_query, head_key, head_value = inputs
        scores = jnp.dot(head_query, head_key.T, preferred_element_type=jnp.float32) * softmax_scale
        row_max = lax.optimization_barrier(jnp.max(scores, axis=-1, keepdims=True))
        weights = jnp.exp(scores - row_max)
        row_sum = lax.optimization_barrier(jnp.sum(weights, axis=-1, keepdims=True))
        attended = jnp.dot(weights.astype(jnp.bfloat16), head_value, preferred_element_type=jnp.float32)
        return (attended / row_sum).astype(jnp.bfloat16)
    cross_heads = lax.map(cross_head, (cross_heads_in, text_keys, text_values))
    cross_out = cross_heads.transpose(1, 0, 2).reshape(TOKENS, H * HD)
    return (self_out, cross_out)
```

```python
import functools
import math

import jax
import jax.numpy as jnp
from jax import lax
from jax.experimental import pallas as pl
from jax.experimental.pallas import tpu as pltpu
from jax.sharding import PartitionSpec as P

SB = 16
LOG2_E = 1.4426950408889634


def pack_kernel(order_ref, query_ref, key_ref, value_ref, out_ref, *, head_dim):
    devices, per_run = out_ref.shape[:2]
    sources = (query_ref, key_ref, value_ref)

    def fill(slot, carry):
        target = slot // per_run
        run = slot % per_run
        head = jnp.maximum(order_ref[slot], 0)
        columns = pl.ds(pl.multiple_of(head * head_dim, head_dim), head_dim)
        for index, source in enumerate(sources):
            out_ref[target, run, index] = source[:, columns]
        return carry

    lax.fori_loop(0, devices * per_run, fill, 0)


def unpack_kernel(order_ref, returned_ref, out_ref, *, head_dim):
    devices, per_run = returned_ref.shape[:2]

    def fill(slot, carry):
        head = order_ref[slot]

        @pl.when(head >= 0)
        def _():
            columns = pl.ds(pl.multiple_of(head * head_dim, head_dim), head_dim)
            out_ref[:, columns] = returned_ref[slot // per_run, slot % per_run]

        return carry

    lax.fori_loop(0, devices * per_run, fill, 0)


def attend_tile(tile, width, band, data_ref, out_ref, score_ref, scale):
    stripe_len, _, _, rows, head_dim = data_ref.shape
    start = jnp.clip(2 * tile - band, 0, stripe_len - width)
    query = data_ref[pl.ds(2 * tile, 2), 0, 0].reshape(2 * rows, head_dim)
    peak = None
    for chunk in range(0, width, 2):
        keys = data_ref[pl.ds(start + chunk, 2), 0, 1].reshape(2 * rows, head_dim)
        scores = lax.dot_general(
            query, keys, (((1,), (1,)), ((), ())), preferred_element_type=jnp.float32
        )
        for part in range(2):
            key_block = start + chunk + part
            halves = []
            for half in range(2):
                outside = jnp.abs(2 * tile + half - key_block) > band
                bias = jnp.where(outside, -jnp.inf, 0.0).astype(jnp.float32)
                halves.append(
                    scores[half * rows : (half + 1) * rows, part * rows : (part + 1) * rows] + bias
                )
            masked = jnp.concatenate(halves, axis=0)
            score_ref[:, (chunk + part) * rows : (chunk + part + 1) * rows] = masked
            peak = masked if peak is None else jnp.maximum(peak, masked)
    peak = jnp.max(peak, axis=1, keepdims=True)
    total = None
    running = None
    for chunk in range(0, width, 2):
        weights = jnp.exp2(
            (score_ref[:, chunk * rows : (chunk + 2) * rows] - peak) * (scale * LOG2_E)
        )
        values = data_ref[pl.ds(start + chunk, 2), 0, 2].reshape(2 * rows, head_dim)
        partial = weights[:, :rows] + weights[:, rows:]
        product = jnp.dot(
            weights.astype(jnp.bfloat16), values, preferred_element_type=jnp.float32
        )
        total = partial if total is None else total + partial
        running = product if running is None else running + product
    total = jnp.sum(total, axis=1, keepdims=True)
    out_ref[pl.ds(2 * tile, 2), 0] = (
        (running / total).astype(jnp.bfloat16).reshape(2, rows, head_dim)
    )


def attend_kernel(band_ref, data_ref, out_ref, score_ref, *, scale):
    stripe_len = data_ref.shape[0]
    band = band_ref[pl.program_id(0)]

    def step(tile, carry):
        low = jnp.maximum(2 * tile - band, 0)
        high = jnp.minimum(2 * tile + 1 + band, stripe_len - 1)
        quarter = stripe_len // 4
        level = (high - low) // quarter
        for index in range(4):

            @pl.when(level == index)
            def _():
                attend_tile(
                    tile, (index + 1) * quarter, band, data_ref, out_ref, score_ref, scale
                )

        return carry

    @pl.when(band >= 0)
    def _():
        lax.fori_loop(0, stripe_len // 2, step, 0)


def cross_kernel(query_ref, key_ref, value_ref, out_ref, *, head_dim, scale, group):
    def step(index, carry):
        for offset in range(group):
            head = index * group + offset
            columns = pl.ds(pl.multiple_of(head * head_dim, head_dim), head_dim)
            scores = lax.dot_general(
                query_ref[:, columns],
                key_ref[:, columns],
                (((1,), (1,)), ((), ())),
                preferred_element_type=jnp.float32,
            )
            peak = jnp.max(scores, axis=1, keepdims=True)
            weights = jnp.exp2((scores - peak) * (scale * LOG2_E))
            total = jnp.sum(weights, axis=1, keepdims=True)
            running = jnp.dot(
                weights.astype(jnp.bfloat16),
                value_ref[:, columns],
                preferred_element_type=jnp.float32,
            )
            out_ref[:, columns] = (running / total).astype(jnp.bfloat16)
        return carry

    lax.fori_loop(0, query_ref.shape[1] // head_dim // group, step, 0)


def stripe_groups(devices):
    return [list(range(first, first + SB)) for first in range(0, devices, SB)]


def shards(
    self_query, self_key, self_value, cross_query, context, key_weight, value_weight, band_width
):
    devices = lax.axis_size("seq")
    device = lax.axis_index("seq")
    tok_rows, width = self_query.shape
    head_count = band_width.shape[0]
    head_dim = width // head_count
    scale = 1.0 / math.sqrt(head_dim)
    groups = stripe_groups(devices)
    per_run = (head_count + SB - 1) // SB
    slot_total = SB * per_run

    head_ids = jnp.arange(head_count, dtype=jnp.int32)
    ahead = (band_width[None, :] > band_width[:, None]) | (
        (band_width[None, :] == band_width[:, None]) & (head_ids[None, :] < head_ids[:, None])
    )
    rank = jnp.sum(ahead.astype(jnp.int32), axis=1)
    slot_ids = jnp.arange(slot_total, dtype=jnp.int32)
    run, seat = slot_ids % per_run, slot_ids // per_run
    slot_rank = run * SB + jnp.where(run % 2 == 0, seat, SB - 1 - seat)
    hits = slot_rank[:, None] == rank[None, :]
    order = jnp.sum(jnp.where(hits, head_ids[None, :] + 1, 0), axis=1) - 1
    bands = jnp.sum(jnp.where(hits, band_width[None, :] + 1, 0), axis=1) - 1
    own_bands = lax.dynamic_slice_in_dim(bands, (device % SB) * per_run, per_run)

    vmem = pl.BlockSpec(memory_space=pltpu.VMEM)
    smem = pl.BlockSpec(memory_space=pltpu.SMEM)
    outgoing = pl.pallas_call(
        functools.partial(pack_kernel, head_dim=head_dim),
        out_shape=jax.ShapeDtypeStruct((SB, per_run, 3, tok_rows, head_dim), jnp.bfloat16),
        in_specs=[smem, vmem, vmem, vmem],
        out_specs=vmem,
        name="pack",
    )(order, self_query, self_key, self_value)
    arrived = lax.all_to_all(
        outgoing, "seq", split_axis=0, concat_axis=0, tiled=True, axis_index_groups=groups
    )
    results = pl.pallas_call(
        functools.partial(attend_kernel, scale=scale),
        out_shape=jax.ShapeDtypeStruct((SB, per_run, tok_rows, head_dim), jnp.bfloat16),
        grid_spec=pltpu.PrefetchScalarGridSpec(
            num_scalar_prefetch=1,
            grid=(per_run,),
            in_specs=[
                pl.BlockSpec(
                    (SB, 1, 3, tok_rows, head_dim), lambda run, bands: (0, run, 0, 0, 0)
                )
            ],
            out_specs=pl.BlockSpec(
                (SB, 1, tok_rows, head_dim), lambda run, bands: (0, run, 0, 0)
            ),
            scratch_shapes=[pltpu.VMEM((2 * tok_rows, SB * tok_rows), jnp.float32)],
        ),
        name="attend",
    )(own_bands, arrived)
    returned = lax.all_to_all(
        results, "seq", split_axis=0, concat_axis=0, tiled=True, axis_index_groups=groups
    )
    self_out = pl.pallas_call(
        functools.partial(unpack_kernel, head_dim=head_dim),
        out_shape=jax.ShapeDtypeStruct((tok_rows, width), jnp.bfloat16),
        in_specs=[smem, vmem],
        out_specs=vmem,
        name="unpack",
    )(order, returned)

    text_key = jnp.dot(context, key_weight, preferred_element_type=jnp.float32).astype(jnp.bfloat16)
    text_value = jnp.dot(context, value_weight, preferred_element_type=jnp.float32).astype(
        jnp.bfloat16
    )
    text_key = lax.all_gather(text_key, "seq", axis=1, tiled=True)
    text_value = lax.all_gather(text_value, "seq", axis=1, tiled=True)
    cross_out = pl.pallas_call(
        functools.partial(cross_kernel, head_dim=head_dim, scale=scale, group=4),
        out_shape=jax.ShapeDtypeStruct((tok_rows, width), jnp.bfloat16),
        in_specs=[vmem, vmem, vmem],
        out_specs=vmem,
        name="cross",
    )(cross_query, text_key, text_value)
    return (self_out, cross_out)


def solution(mesh):
    in_specs = (
        P(("groups", "seq"), None),
        P(("groups", "seq"), None),
        P(("groups", "seq"), None),
        P(("groups", "seq"), None),
        P("groups", None),
        P(None, "seq"),
        P(None, "seq"),
        P(),
    )
    out_specs = (P(("groups", "seq"), None), P(("groups", "seq"), None))
    return jax.shard_map(shards, mesh=mesh, in_specs=in_specs, out_specs=out_specs, check_vma=False)
```

```python
import functools
import math

import jax
import jax.numpy as jnp
from jax import lax
from jax.experimental import pallas as pl
from jax.experimental.pallas import tpu as pltpu
from jax.sharding import PartitionSpec as P

SB = 16
SEATS = 4
REACH = 3
LOG2_E = 1.4426950408889634


def pack_kernel(*refs, head_dim):
    query_ref, key_ref, value_ref = sources = refs[-5:-2] if len(refs) == 7 else refs[-4:-1]
    orders, outs = (refs[:2], refs[-2:]) if len(refs) == 7 else (refs[:1], refs[-1:])
    del query_ref, key_ref, value_ref
    for order_ref, out_ref in zip(orders, outs):
        per_run = out_ref.shape[2]

        def fill(slot, carry, order_ref=order_ref, out_ref=out_ref, per_run=per_run):
            head = jnp.maximum(order_ref[slot], 0)
            columns = pl.ds(pl.multiple_of(head * head_dim, head_dim), head_dim)
            for index, source in enumerate(sources):
                out_ref[slot // per_run, index, slot % per_run] = source[:, columns]
            return carry

        lax.fori_loop(0, out_ref.shape[0] * per_run, fill, 0)


def unpack_kernel(*refs, head_dim):
    count = len(refs) // 2
    out_ref = refs[-1]
    for order_ref, returned_ref in zip(refs[:count], refs[count:-1]):
        per_run = returned_ref.shape[1]

        def fill(slot, carry, order_ref=order_ref, returned_ref=returned_ref, per_run=per_run):
            head = order_ref[slot]

            @pl.when(head >= 0)
            def _():
                columns = pl.ds(pl.multiple_of(head * head_dim, head_dim), head_dim)
                out_ref[:, columns] = returned_ref[slot // per_run, slot % per_run]

            return carry

        lax.fori_loop(0, returned_ref.shape[0] * per_run, fill, 0)


def attend_tile(tile, width, band, data_ref, out_ref, score_ref, scale):
    stripe_len, _, _, rows, head_dim = data_ref.shape
    start = jnp.clip(2 * tile - band, 0, stripe_len - width)
    query = data_ref[pl.ds(2 * tile, 2), 0, 0].reshape(2 * rows, head_dim)
    peak = None
    for chunk in range(0, width, 2):
        keys = data_ref[pl.ds(start + chunk, 2), 1, 0].reshape(2 * rows, head_dim)
        scores = lax.dot_general(
            query, keys, (((1,), (1,)), ((), ())), preferred_element_type=jnp.float32
        )
        for part in range(2):
            key_block = start + chunk + part
            halves = []
            for half in range(2):
                outside = jnp.abs(2 * tile + half - key_block) > band
                bias = jnp.where(outside, -jnp.inf, 0.0).astype(jnp.float32)
                halves.append(
                    scores[half * rows : (half + 1) * rows, part * rows : (part + 1) * rows] + bias
                )
            masked = jnp.concatenate(halves, axis=0)
            score_ref[:, (chunk + part) * rows : (chunk + part + 1) * rows] = masked
            peak = masked if peak is None else jnp.maximum(peak, masked)
    peak = jnp.max(peak, axis=1, keepdims=True)
    total = None
    running = None
    for chunk in range(0, width, 2):
        weights = jnp.exp2(
            (score_ref[:, chunk * rows : (chunk + 2) * rows] - peak) * (scale * LOG2_E)
        )
        values = data_ref[pl.ds(start + chunk, 2), 2, 0].reshape(2 * rows, head_dim)
        partial = weights[:, :rows] + weights[:, rows:]
        product = jnp.dot(
            weights.astype(jnp.bfloat16), values, preferred_element_type=jnp.float32
        )
        total = partial if total is None else total + partial
        running = product if running is None else running + product
    total = jnp.sum(total, axis=1, keepdims=True)
    out_ref[pl.ds(2 * tile, 2), 0] = (
        (running / total).astype(jnp.bfloat16).reshape(2, rows, head_dim)
    )


def attend_kernel(band_ref, data_ref, out_ref, score_ref, *, scale):
    stripe_len = data_ref.shape[0]
    band = band_ref[pl.program_id(0)]

    def step(tile, carry):
        low = jnp.maximum(2 * tile - band, 0)
        high = jnp.minimum(2 * tile + 1 + band, stripe_len - 1)
        quarter = stripe_len // 4
        level = (high - low) // quarter
        for index in range(4):

            @pl.when(level == index)
            def _():
                attend_tile(
                    tile, (index + 1) * quarter, band, data_ref, out_ref, score_ref, scale
                )

        return carry

    @pl.when(band >= 0)
    def _():
        lax.fori_loop(0, stripe_len // 2, step, 0)


def cross_kernel(query_ref, key_ref, value_ref, out_ref, *, head_dim, scale, group):
    def step(index, carry):
        for offset in range(group):
            head = index * group + offset
            columns = pl.ds(pl.multiple_of(head * head_dim, head_dim), head_dim)
            scores = lax.dot_general(
                query_ref[:, columns],
                key_ref[:, columns],
                (((1,), (1,)), ((), ())),
                preferred_element_type=jnp.float32,
            )
            peak = jnp.max(scores, axis=1, keepdims=True)
            weights = jnp.exp2((scores - peak) * (scale * LOG2_E))
            total = jnp.sum(weights, axis=1, keepdims=True)
            running = jnp.dot(
                weights.astype(jnp.bfloat16),
                value_ref[:, columns],
                preferred_element_type=jnp.float32,
            )
            out_ref[:, columns] = (running / total).astype(jnp.bfloat16)
        return carry

    lax.fori_loop(0, query_ref.shape[1] // head_dim // group, step, 0)


def narrow_kernel(band_ref, place_ref, own_ref, low_ref, high_ref, out_ref, *, scale, reach):
    seats, _, per_run, rows, head_dim = own_ref.shape
    first = place_ref[0]

    def block_of(part, place, run):
        if place < reach:
            return low_ref[place, part, run]
        if place < reach + seats:
            return own_ref[place - reach, part + 1, run]
        return high_ref[place - reach - seats, part, run]

    def step(run, carry):
        band = band_ref[run]
        for seat in range(seats):
            query = own_ref[seat, 0, run]
            tiles = []
            for place in range(seat, seat + 2 * reach + 1):
                scores = lax.dot_general(
                    query,
                    block_of(0, place, run),
                    (((1,), (1,)), ((), ())),
                    preferred_element_type=jnp.float32,
                )
                if place != seat + reach:
                    block = first + place - reach
                    outside = (abs(place - seat - reach) > band) | (block < 0) | (block >= SB)
                    scores = scores + jnp.where(outside, -jnp.inf, 0.0).astype(jnp.float32)
                tiles.append(scores)
            peak = jnp.max(functools.reduce(jnp.maximum, tiles), axis=1, keepdims=True)
            total, running = 0.0, 0.0
            for place, scores in enumerate(tiles, seat):
                weights = jnp.exp2((scores - peak) * (scale * LOG2_E))
                total = total + weights
                running = running + jnp.dot(
                    weights.astype(jnp.bfloat16),
                    block_of(1, place, run),
                    preferred_element_type=jnp.float32,
                )
            total = jnp.sum(total, axis=1, keepdims=True)
            out_ref[seat, run] = (running / total).astype(jnp.bfloat16)
        return carry

    lax.fori_loop(0, per_run, step, 0)


def cross_pairs_kernel(place_ref, query_ref, mine_ref, other_ref, out_ref, *, head_dim, scale):
    entries, _, pair_width = mine_ref.shape
    bits = entries.bit_length() - 1

    def attend(key_ref, value_ref):
        def step(entry, carry):
            pair = place_ref[0]
            for bit in range(bits):
                pair = pair ^ (((entry >> bit) & 1) << (bits - 1 - bit))
            for offset in range(pair_width // head_dim):
                source = pl.ds(offset * head_dim, head_dim)
                target = pl.ds(
                    pl.multiple_of(pair * pair_width + offset * head_dim, head_dim), head_dim
                )
                scores = lax.dot_general(
                    query_ref[:, target],
                    key_ref[entry, :, source],
                    (((1,), (1,)), ((), ())),
                    preferred_element_type=jnp.float32,
                )
                peak = jnp.max(scores, axis=1, keepdims=True)
                weights = jnp.exp2((scores - peak) * (scale * LOG2_E))
                total = jnp.sum(weights, axis=1, keepdims=True)
                running = jnp.dot(
                    weights.astype(jnp.bfloat16),
                    value_ref[entry, :, source],
                    preferred_element_type=jnp.float32,
                )
                out_ref[:, target] = (running / total).astype(jnp.bfloat16)
            return carry

        lax.fori_loop(0, entries, step, 0)

    @pl.when(place_ref[1] == 0)
    def _():
        attend(mine_ref, other_ref)

    @pl.when(place_ref[1] == 1)
    def _():
        attend(other_ref, mine_ref)


def swap(values, distance):
    devices = lax.axis_size("seq")
    return lax.ppermute(values, "seq", [(source, source ^ distance) for source in range(devices)])


def cross_attention(cross_query, context, key_weight, value_weight, head_dim, scale):
    devices = lax.axis_size("seq")
    device = lax.axis_index("seq")
    tok_rows, width = cross_query.shape
    text_len = context.shape[0]
    text_key = jnp.dot(context, key_weight, preferred_element_type=jnp.float32).astype(jnp.bfloat16)
    text_value = jnp.dot(context, value_weight, preferred_element_type=jnp.float32).astype(
        jnp.bfloat16
    )
    out_shape = jax.ShapeDtypeStruct((tok_rows, width), jnp.bfloat16)
    vmem = pl.BlockSpec(memory_space=pltpu.VMEM)
    smem = pl.BlockSpec(memory_space=pltpu.SMEM)
    pair_width = 2 * key_weight.shape[1]
    if pair_width % head_dim or devices & (devices - 1):
        return pl.pallas_call(
            functools.partial(cross_kernel, head_dim=head_dim, scale=scale, group=4),
            out_shape=out_shape,
            in_specs=[vmem, vmem, vmem],
            out_specs=vmem,
            name="cross",
        )(
            cross_query,
            lax.all_gather(text_key, "seq", axis=1, tiled=True),
            lax.all_gather(text_value, "seq", axis=1, tiled=True),
        )
    even = device % 2 == 0
    kept = jnp.where(even, text_key, text_value)
    came = swap(jnp.where(even, text_value, text_key), 1)
    mine = jnp.where(
        even, jnp.concatenate([kept, came], axis=1), jnp.concatenate([came, kept], axis=1)
    ).reshape(1, text_len, pair_width)
    distance = devices // 2
    while distance > 1:
        mine = jnp.concatenate([mine, swap(mine, distance)], axis=0)
        distance //= 2
    other = swap(mine, 1)
    place = jnp.stack([device // 2, device % 2]).astype(jnp.int32)
    return pl.pallas_call(
        functools.partial(cross_pairs_kernel, head_dim=head_dim, scale=scale),
        out_shape=out_shape,
        in_specs=[smem, vmem, vmem, vmem],
        out_specs=vmem,
        name="cross",
    )(place, cross_query, mine, other)


def deal(rank, band_width, first, seats, per_run):
    slot_ids = jnp.arange(seats * per_run, dtype=jnp.int32)
    run, seat = slot_ids % per_run, slot_ids // per_run
    wanted = first + run * seats + jnp.where(run % 2 == 0, seat, seats - 1 - seat)
    hits = wanted[:, None] == rank[None, :]
    head_ids = jnp.arange(rank.shape[0], dtype=jnp.int32)
    order = jnp.sum(jnp.where(hits, head_ids[None, :] + 1, 0), axis=1) - 1
    bands = jnp.sum(jnp.where(hits, band_width[None, :] + 1, 0), axis=1) - 1
    return order, bands


def index_groups(devices, size):
    return [list(range(first, first + size)) for first in range(0, devices, size)]


def attention(rank, per_run, narrow_run, arrays):
    (self_query, self_key, self_value, cross_query, context, key_weight, value_weight, band_width) = (
        arrays
    )
    devices = lax.axis_size("seq")
    device = lax.axis_index("seq")
    tok_rows, width = self_query.shape
    head_count = band_width.shape[0]
    head_dim = width // head_count
    scale = 1.0 / math.sqrt(head_dim)
    vmem = pl.BlockSpec(memory_space=pltpu.VMEM)
    smem = pl.BlockSpec(memory_space=pltpu.SMEM)

    deals = [deal(rank, band_width, 0, SB, per_run)]
    shapes = [(SB, 3, per_run, tok_rows, head_dim)]
    if narrow_run:
        deals.append(deal(rank, band_width, SB * per_run, SEATS, narrow_run))
        shapes.append((SEATS, 3, narrow_run, tok_rows, head_dim))
    packed = pl.pallas_call(
        functools.partial(pack_kernel, head_dim=head_dim),
        out_shape=[jax.ShapeDtypeStruct(shape, jnp.bfloat16) for shape in shapes],
        in_specs=[smem] * len(deals) + [vmem] * 3,
        out_specs=[vmem] * len(deals),
        name="pack",
    )(*[order for order, _ in deals], self_query, self_key, self_value)

    def exchange(values, size):
        return lax.all_to_all(
            values,
            "seq",
            split_axis=0,
            concat_axis=0,
            tiled=True,
            axis_index_groups=index_groups(devices, size),
        )

    arrived = exchange(packed[0], SB)
    own_bands = lax.dynamic_slice_in_dim(deals[0][1], (device % SB) * per_run, per_run)
    results = pl.pallas_call(
        functools.partial(attend_kernel, scale=scale),
        out_shape=jax.ShapeDtypeStruct((SB, per_run, tok_rows, head_dim), jnp.bfloat16),
        grid_spec=pltpu.PrefetchScalarGridSpec(
            num_scalar_prefetch=1,
            grid=(per_run,),
            in_specs=[
                pl.BlockSpec(
                    (SB, 3, 1, tok_rows, head_dim), lambda run, bands: (0, 0, run, 0, 0)
                )
            ],
            out_specs=pl.BlockSpec(
                (SB, 1, tok_rows, head_dim), lambda run, bands: (0, run, 0, 0)
            ),
            scratch_shapes=[pltpu.VMEM((2 * tok_rows, SB * tok_rows), jnp.float32)],
        ),
        name="attend",
    )(own_bands, arrived)
    returned = [exchange(results, SB)]
    if narrow_run:
        own = exchange(packed[1], SEATS)
        upward = [
            (source, source + SEATS)
            for source in range(devices - SEATS)
            if source // SB == (source + SEATS) // SB
        ]
        low = lax.ppermute(own[SEATS - REACH :, 1:], "seq", upward)
        high = lax.ppermute(own[:REACH, 1:], "seq", [(target, source) for source, target in upward])
        narrow_bands = lax.dynamic_slice_in_dim(
            deals[1][1], (device % SEATS) * narrow_run, narrow_run
        )
        first = jnp.reshape(device % SB // SEATS * SEATS, (1,)).astype(jnp.int32)
        narrow = pl.pallas_call(
            functools.partial(narrow_kernel, scale=scale, reach=REACH),
            out_shape=jax.ShapeDtypeStruct((SEATS, narrow_run, tok_rows, head_dim), jnp.bfloat16),
            in_specs=[smem, smem, vmem, vmem, vmem],
            out_specs=vmem,
            name="narrow",
        )(narrow_bands, first, own, low, high)
        returned.append(exchange(narrow, SEATS))
    self_out = pl.pallas_call(
        functools.partial(unpack_kernel, head_dim=head_dim),
        out_shape=jax.ShapeDtypeStruct((tok_rows, width), jnp.bfloat16),
        in_specs=[smem] * len(deals) + [vmem] * len(deals),
        out_specs=vmem,
        name="unpack",
    )(*[order for order, _ in deals], *returned)
    cross_out = cross_attention(cross_query, context, key_weight, value_weight, head_dim, scale)
    return (self_out, cross_out)


def shards(*arrays):
    band_width = arrays[-1]
    head_count = band_width.shape[0]
    head_ids = jnp.arange(head_count, dtype=jnp.int32)
    ahead = (band_width[None, :] > band_width[:, None]) | (
        (band_width[None, :] == band_width[:, None]) & (head_ids[None, :] < head_ids[:, None])
    )
    rank = jnp.sum(ahead.astype(jnp.int32), axis=1)
    whole_run = head_count // SB
    narrow_count = head_count - whole_run * SB
    narrow_run = (narrow_count + SEATS - 1) // SEATS
    if not narrow_count or not whole_run:
        return attention(rank, (head_count + SB - 1) // SB, 0, arrays)
    close = jnp.sum((band_width <= REACH).astype(jnp.int32)) >= narrow_count
    return lax.cond(
        close,
        functools.partial(attention, rank, whole_run, narrow_run),
        functools.partial(attention, rank, whole_run + 1, 0),
        arrays,
    )


def solution(mesh):
    in_specs = (
        P(("groups", "seq"), None),
        P(("groups", "seq"), None),
        P(("groups", "seq"), None),
        P(("groups", "seq"), None),
        P("groups", None),
        P(None, "seq"),
        P(None, "seq"),
        P(),
    )
    out_specs = (P(("groups", "seq"), None), P(("groups", "seq"), None))
    return jax.shard_map(shards, mesh=mesh, in_specs=in_specs, out_specs=out_specs, check_vma=False)
```

```python
import functools
import math

import jax
import jax.numpy as jnp
from jax import lax
from jax.experimental import pallas as pl
from jax.experimental.pallas import tpu as pltpu
from jax.sharding import PartitionSpec as P


SB = 16
SEATS = 4
REACH = 3
LOG2_E = 1.4426950408889634


def pack_kernel(*refs, head_dim):
    query_ref, key_ref, value_ref = sources = refs[-5:-2] if len(refs) == 7 else refs[-4:-1]
    orders, outs = (refs[:2], refs[-2:]) if len(refs) == 7 else (refs[:1], refs[-1:])
    del query_ref, key_ref, value_ref
    for order_ref, out_ref in zip(orders, outs):
        per_run = out_ref.shape[2]

        def fill(slot, carry, order_ref=order_ref, out_ref=out_ref, per_run=per_run):
            head = jnp.maximum(order_ref[slot], 0)
            columns = pl.ds(pl.multiple_of(head * head_dim, head_dim), head_dim)
            for index, source in enumerate(sources):
                out_ref[slot // per_run, index, slot % per_run] = source[:, columns]
            return carry

        lax.fori_loop(0, out_ref.shape[0] * per_run, fill, 0)


def unpack_kernel(*refs, head_dim):
    count = len(refs) // 2
    out_ref = refs[-1]
    for order_ref, returned_ref in zip(refs[:count], refs[count:-1]):
        per_run = returned_ref.shape[1]

        def fill(slot, carry, order_ref=order_ref, returned_ref=returned_ref, per_run=per_run):
            head = order_ref[slot]

            @pl.when(head >= 0)
            def _():
                columns = pl.ds(pl.multiple_of(head * head_dim, head_dim), head_dim)
                out_ref[:, columns] = returned_ref[slot // per_run, slot % per_run]

            return carry

        lax.fori_loop(0, returned_ref.shape[0] * per_run, fill, 0)


def attend_tile(tile, width, band, data_ref, out_ref, score_ref, scale):
    stripe_len, _, _, rows, head_dim = data_ref.shape
    start = jnp.clip(2 * tile - band, 0, stripe_len - width)
    query = data_ref[pl.ds(2 * tile, 2), 0, 0].reshape(2 * rows, head_dim)
    peak = None
    for chunk in range(0, width, 2):
        keys = data_ref[pl.ds(start + chunk, 2), 1, 0].reshape(2 * rows, head_dim)
        scores = lax.dot_general(
            query, keys, (((1,), (1,)), ((), ())), preferred_element_type=jnp.float32
        )
        for part in range(2):
            key_block = start + chunk + part
            halves = []
            for half in range(2):
                outside = jnp.abs(2 * tile + half - key_block) > band
                bias = jnp.where(outside, -jnp.inf, 0.0).astype(jnp.float32)
                halves.append(
                    scores[half * rows : (half + 1) * rows, part * rows : (part + 1) * rows] + bias
                )
            masked = jnp.concatenate(halves, axis=0)
            score_ref[:, (chunk + part) * rows : (chunk + part + 1) * rows] = masked
            peak = masked if peak is None else jnp.maximum(peak, masked)
    peak = jnp.max(peak, axis=1, keepdims=True)
    total = None
    running = None
    for chunk in range(0, width, 2):
        weights = jnp.exp2(
            (score_ref[:, chunk * rows : (chunk + 2) * rows] - peak) * (scale * LOG2_E)
        )
        values = data_ref[pl.ds(start + chunk, 2), 2, 0].reshape(2 * rows, head_dim)
        partial = weights[:, :rows] + weights[:, rows:]
        product = jnp.dot(
            weights.astype(jnp.bfloat16), values, preferred_element_type=jnp.float32
        )
        total = partial if total is None else total + partial
        running = product if running is None else running + product
    total = jnp.sum(total, axis=1, keepdims=True)
    out_ref[pl.ds(2 * tile, 2), 0] = (
        (running / total).astype(jnp.bfloat16).reshape(2, rows, head_dim)
    )


def attend_kernel(band_ref, data_ref, out_ref, score_ref, *, scale):
    stripe_len = data_ref.shape[0]
    band = band_ref[pl.program_id(0)]

    def step(tile, carry):
        low = jnp.maximum(2 * tile - band, 0)
        high = jnp.minimum(2 * tile + 1 + band, stripe_len - 1)
        quarter = stripe_len // 4
        level = (high - low) // quarter
        for index in range(4):

            @pl.when(level == index)
            def _():
                attend_tile(
                    tile, (index + 1) * quarter, band, data_ref, out_ref, score_ref, scale
                )

        return carry

    @pl.when(band >= 0)
    def _():
        lax.fori_loop(0, stripe_len // 2, step, 0)


def cross_kernel(query_ref, key_ref, value_ref, out_ref, *, head_dim, scale, group):
    def step(index, carry):
        for offset in range(group):
            head = index * group + offset
            columns = pl.ds(pl.multiple_of(head * head_dim, head_dim), head_dim)
            scores = lax.dot_general(
                query_ref[:, columns],
                key_ref[:, columns],
                (((1,), (1,)), ((), ())),
                preferred_element_type=jnp.float32,
            )
            peak = jnp.max(scores, axis=1, keepdims=True)
            weights = jnp.exp2((scores - peak) * (scale * LOG2_E))
            total = jnp.sum(weights, axis=1, keepdims=True)
            running = jnp.dot(
                weights.astype(jnp.bfloat16),
                value_ref[:, columns],
                preferred_element_type=jnp.float32,
            )
            out_ref[:, columns] = (running / total).astype(jnp.bfloat16)
        return carry

    lax.fori_loop(0, query_ref.shape[1] // head_dim // group, step, 0)


def narrow_kernel(band_ref, place_ref, own_ref, low_ref, high_ref, out_ref, *, scale, reach):
    seats, _, per_run, _, _ = own_ref.shape
    first = place_ref[0]

    def block_of(part, place, run):
        if place < reach:
            return low_ref[place, part, run]
        if place < reach + seats:
            return own_ref[place - reach, part + 1, run]
        return high_ref[place - reach - seats, part, run]

    def step(run, carry):
        band = band_ref[run]
        for seat in range(seats):
            query = own_ref[seat, 0, run]
            tiles = []
            for place in range(seat, seat + 2 * reach + 1):
                scores = lax.dot_general(
                    query,
                    block_of(0, place, run),
                    (((1,), (1,)), ((), ())),
                    preferred_element_type=jnp.float32,
                )
                if place != seat + reach:
                    block = first + place - reach
                    outside = (abs(place - seat - reach) > band) | (block < 0) | (block >= SB)
                    scores = scores + jnp.where(outside, -jnp.inf, 0.0).astype(jnp.float32)
                tiles.append(scores)
            peak = jnp.max(functools.reduce(jnp.maximum, tiles), axis=1, keepdims=True)
            total, running = 0.0, 0.0
            for place, scores in enumerate(tiles, seat):
                weights = jnp.exp2((scores - peak) * (scale * LOG2_E))
                total = total + weights
                running = running + jnp.dot(
                    weights.astype(jnp.bfloat16),
                    block_of(1, place, run),
                    preferred_element_type=jnp.float32,
                )
            total = jnp.sum(total, axis=1, keepdims=True)
            out_ref[seat, run] = (running / total).astype(jnp.bfloat16)
        return carry

    lax.fori_loop(0, per_run, step, 0)


def project_kernel(context_ref, key_ref, value_ref, out_ref, total_ref):
    weights = jnp.concatenate([key_ref[...], value_ref[...]], axis=0)
    product = lax.dot_general(
        context_ref[...], weights, (((1,), (1,)), ((), ())), preferred_element_type=jnp.float32
    )

    @pl.when(pl.program_id(0) == 0)
    def _():
        total_ref[...] = product

    @pl.when(pl.program_id(0) > 0)
    def _():
        total_ref[...] += product

    @pl.when(pl.program_id(0) == pl.num_programs(0) - 1)
    def _():
        out_ref[0] = total_ref[...].astype(jnp.bfloat16)


def project(context, key_weight, value_weight, steps=4):
    text_len, depth = context.shape
    columns = key_weight.shape[1]
    part = depth // steps
    weight_spec = pl.BlockSpec((columns, part), lambda step: (0, step))
    return pl.pallas_call(
        project_kernel,
        out_shape=jax.ShapeDtypeStruct((1, text_len, 2 * columns), jnp.bfloat16),
        grid=(steps,),
        in_specs=[
            pl.BlockSpec((text_len, part), lambda step: (0, step)),
            weight_spec,
            weight_spec,
        ],
        out_specs=pl.BlockSpec((1, text_len, 2 * columns), lambda step: (0, 0, 0)),
        scratch_shapes=[pltpu.VMEM((text_len, 2 * columns), jnp.float32)],
        name="project",
    )(context, key_weight.T, value_weight.T)


def cross_pairs_kernel(
    place_ref, query_ref, mine_ref, other_ref, out_ref, key_ref, value_ref, *, head_dim, scale
):
    entries, _, pair_width = mine_ref.shape
    columns = pair_width // 2
    bits = entries.bit_length() - 1

    def attend(even_ref, odd_ref):
        def step(entry, carry):
            pair = place_ref[0]
            for bit in range(bits):
                pair = pair ^ (((entry >> bit) & 1) << (bits - 1 - bit))
            key_ref[:, :columns] = even_ref[entry, :, :columns]
            key_ref[:, columns:] = odd_ref[entry, :, :columns]
            value_ref[:, :columns] = even_ref[entry, :, columns:]
            value_ref[:, columns:] = odd_ref[entry, :, columns:]
            for offset in range(pair_width // head_dim):
                source = pl.ds(offset * head_dim, head_dim)
                target = pl.ds(
                    pl.multiple_of(pair * pair_width + offset * head_dim, head_dim), head_dim
                )
                scores = lax.dot_general(
                    query_ref[:, target],
                    key_ref[:, source],
                    (((1,), (1,)), ((), ())),
                    preferred_element_type=jnp.float32,
                )
                peak = jnp.max(scores, axis=1, keepdims=True)
                weights = jnp.exp2((scores - peak) * (scale * LOG2_E))
                total = jnp.sum(weights, axis=1, keepdims=True)
                running = jnp.dot(
                    weights.astype(jnp.bfloat16),
                    value_ref[:, source],
                    preferred_element_type=jnp.float32,
                )
                out_ref[:, target] = (running / total).astype(jnp.bfloat16)
            return carry

        lax.fori_loop(0, entries, step, 0)

    @pl.when(place_ref[1] == 0)
    def _():
        attend(mine_ref, other_ref)

    @pl.when(place_ref[1] == 1)
    def _():
        attend(other_ref, mine_ref)


def swap(values, distance):
    devices = lax.axis_size("seq")
    return lax.ppermute(values, "seq", [(source, source ^ distance) for source in range(devices)])


def doubles(key_weight, head_dim):
    devices = lax.axis_size("seq")
    return (2 * key_weight.shape[1]) % head_dim == 0 and devices & (devices - 1) == 0


def cross_attention(cross_query, context, key_weight, value_weight, head_dim, scale, text):
    devices = lax.axis_size("seq")
    device = lax.axis_index("seq")
    tok_rows, width = cross_query.shape
    out_shape = jax.ShapeDtypeStruct((tok_rows, width), jnp.bfloat16)
    vmem = pl.BlockSpec(memory_space=pltpu.VMEM)
    smem = pl.BlockSpec(memory_space=pltpu.SMEM)
    if text is None:
        text_key = jnp.dot(context, key_weight, preferred_element_type=jnp.float32)
        text_value = jnp.dot(context, value_weight, preferred_element_type=jnp.float32)
        return pl.pallas_call(
            functools.partial(cross_kernel, head_dim=head_dim, scale=scale, group=4),
            out_shape=out_shape,
            in_specs=[vmem, vmem, vmem],
            out_specs=vmem,
            name="cross",
        )(
            cross_query,
            lax.all_gather(text_key.astype(jnp.bfloat16), "seq", axis=1, tiled=True),
            lax.all_gather(text_value.astype(jnp.bfloat16), "seq", axis=1, tiled=True),
        )
    distance = devices // 4
    while distance > 1:
        came = swap(text, distance)
        text = jnp.concatenate([text, came], axis=0)
        distance //= 2
    other = swap(text, 1)
    place = jnp.stack([device // 2, device % 2]).astype(jnp.int32)
    pair = pltpu.VMEM(text.shape[1:], jnp.bfloat16)
    return pl.pallas_call(
        functools.partial(cross_pairs_kernel, head_dim=head_dim, scale=scale),
        out_shape=out_shape,
        in_specs=[smem, vmem, vmem, vmem],
        out_specs=vmem,
        scratch_shapes=[pair, pair],
        name="cross",
    )(place, cross_query, text, other)


def deal(rank, band_width, first, seats, per_run):
    slot_ids = jnp.arange(seats * per_run, dtype=jnp.int32)
    run, seat = slot_ids % per_run, slot_ids // per_run
    wanted = first + run * seats + jnp.where(run % 2 == 0, seat, seats - 1 - seat)
    hits = wanted[:, None] == rank[None, :]
    head_ids = jnp.arange(rank.shape[0], dtype=jnp.int32)
    order = jnp.sum(jnp.where(hits, head_ids[None, :] + 1, 0), axis=1) - 1
    bands = jnp.sum(jnp.where(hits, band_width[None, :] + 1, 0), axis=1) - 1
    return order, bands


def index_groups(devices, size):
    return [list(range(first, first + size)) for first in range(0, devices, size)]


def attention(rank, per_run, narrow_run, arrays):
    (self_query, self_key, self_value, cross_query, context, key_weight, value_weight, band_width) = (
        arrays
    )
    devices = lax.axis_size("seq")
    device = lax.axis_index("seq")
    tok_rows, width = self_query.shape
    head_count = band_width.shape[0]
    head_dim = width // head_count
    scale = 1.0 / math.sqrt(head_dim)
    vmem = pl.BlockSpec(memory_space=pltpu.VMEM)
    smem = pl.BlockSpec(memory_space=pltpu.SMEM)

    text = None
    if doubles(key_weight, head_dim):
        text = project(context, key_weight, value_weight)
        came = swap(text, devices // 2)
    deals = [deal(rank, band_width, 0, SB, per_run)]
    shapes = [(SB, 3, per_run, tok_rows, head_dim)]
    if narrow_run:
        deals.append(deal(rank, band_width, SB * per_run, SEATS, narrow_run))
        shapes.append((SEATS, 3, narrow_run, tok_rows, head_dim))
    packed = pl.pallas_call(
        functools.partial(pack_kernel, head_dim=head_dim),
        out_shape=[jax.ShapeDtypeStruct(shape, jnp.bfloat16) for shape in shapes],
        in_specs=[smem] * len(deals) + [vmem] * 3,
        out_specs=[vmem] * len(deals),
        name="pack",
    )(*[order for order, _ in deals], self_query, self_key, self_value)

    def exchange(values, size):
        return lax.all_to_all(
            values,
            "seq",
            split_axis=0,
            concat_axis=0,
            tiled=True,
            axis_index_groups=index_groups(devices, size),
        )

    outgoing = packed[0]
    if narrow_run:
        own = exchange(packed[1], SEATS)
        upward = [
            (source, source + SEATS)
            for source in range(devices - SEATS)
            if source // SB == (source + SEATS) // SB
        ]
        low = lax.ppermute(own[SEATS - REACH :, 1:], "seq", upward)
        high = lax.ppermute(own[:REACH, 1:], "seq", [(high, low) for low, high in upward])
        if text is not None:
            outgoing, came, own = lax.optimization_barrier((outgoing, came, own))
        else:
            outgoing, own = lax.optimization_barrier((outgoing, own))
    elif text is not None:
        outgoing, came = lax.optimization_barrier((outgoing, came))
    arrived = exchange(outgoing, SB)
    if text is not None:
        text = jnp.concatenate([text, came], axis=0)
    cross_out = cross_attention(
        cross_query, context, key_weight, value_weight, head_dim, scale, text
    )
    own_bands = lax.dynamic_slice_in_dim(deals[0][1], (device % SB) * per_run, per_run)
    results = pl.pallas_call(
        functools.partial(attend_kernel, scale=scale),
        out_shape=jax.ShapeDtypeStruct((SB, per_run, tok_rows, head_dim), jnp.bfloat16),
        grid_spec=pltpu.PrefetchScalarGridSpec(
            num_scalar_prefetch=1,
            grid=(per_run,),
            in_specs=[
                pl.BlockSpec(
                    (SB, 3, 1, tok_rows, head_dim), lambda run, bands: (0, 0, run, 0, 0)
                )
            ],
            out_specs=pl.BlockSpec(
                (SB, 1, tok_rows, head_dim), lambda run, bands: (0, run, 0, 0)
            ),
            scratch_shapes=[pltpu.VMEM((2 * tok_rows, SB * tok_rows), jnp.float32)],
        ),
        name="attend",
    )(own_bands, arrived)
    returned = [exchange(results, SB)]
    if narrow_run:
        narrow_bands = lax.dynamic_slice_in_dim(
            deals[1][1], (device % SEATS) * narrow_run, narrow_run
        )
        first = jnp.reshape(device % SB // SEATS * SEATS, (1,)).astype(jnp.int32)
        narrow = pl.pallas_call(
            functools.partial(narrow_kernel, scale=scale, reach=REACH),
            out_shape=jax.ShapeDtypeStruct((SEATS, narrow_run, tok_rows, head_dim), jnp.bfloat16),
            in_specs=[smem, smem, vmem, vmem, vmem],
            out_specs=vmem,
            name="narrow",
        )(narrow_bands, first, own, low, high)
        returned.append(exchange(narrow, SEATS))
    self_out = pl.pallas_call(
        functools.partial(unpack_kernel, head_dim=head_dim),
        out_shape=jax.ShapeDtypeStruct((tok_rows, width), jnp.bfloat16),
        in_specs=[smem] * len(deals) + [vmem] * len(deals),
        out_specs=vmem,
        name="unpack",
    )(*[order for order, _ in deals], *returned)
    return (self_out, cross_out)


def layer(*arrays):
    band_width = arrays[-1]
    head_count = band_width.shape[0]
    head_ids = jnp.arange(head_count, dtype=jnp.int32)
    ahead = (band_width[None, :] > band_width[:, None]) | (
        (band_width[None, :] == band_width[:, None]) & (head_ids[None, :] < head_ids[:, None])
    )
    rank = jnp.sum(ahead.astype(jnp.int32), axis=1)
    whole_run = head_count // SB
    narrow_count = head_count - whole_run * SB
    narrow_run = (narrow_count + SEATS - 1) // SEATS
    if not narrow_count or not whole_run:
        return attention(rank, (head_count + SB - 1) // SB, 0, arrays)
    close = jnp.sum((band_width <= REACH).astype(jnp.int32)) >= narrow_count
    return lax.cond(
        close,
        functools.partial(attention, rank, whole_run, narrow_run),
        functools.partial(attention, rank, whole_run + 1, 0),
        arrays,
    )


def solution(mesh):
    in_specs = (
        P(("groups", "seq"), None),
        P(("groups", "seq"), None),
        P(("groups", "seq"), None),
        P(("groups", "seq"), None),
        P("groups", None),
        P(None, "seq"),
        P(None, "seq"),
        P(),
    )
    out_specs = (P(("groups", "seq"), None), P(("groups", "seq"), None))
    return jax.shard_map(layer, mesh=mesh, in_specs=in_specs, out_specs=out_specs, check_vma=False)
```

```python
import functools
import math

import jax
import jax.numpy as jnp
from jax import lax
from jax.experimental import pallas as pl
from jax.experimental.pallas import tpu as pltpu
from jax.sharding import PartitionSpec as P


SB = 16
SEATS = 4
REACH = 4
LOG2_E = 1.4426950408889634


def pack_kernel(order_ref, query_ref, key_ref, value_ref, *out_refs, head_dim):
    sources = (query_ref, key_ref, value_ref)
    first = 0
    for out_ref in out_refs:
        seats, _ = out_ref.shape[:2]

        def fill(seat, carry, out_ref=out_ref, first=first):
            head = jnp.maximum(order_ref[first + seat], 0)
            columns = pl.ds(pl.multiple_of(head * head_dim, head_dim), head_dim)
            for index, source in enumerate(sources):
                out_ref[seat, index] = source[:, columns]
            return carry

        lax.fori_loop(0, seats, fill, 0)
        first += seats


def unpack_kernel(order_ref, *refs, head_dim):
    out_ref = refs[-1]
    first = 0
    for returned_ref in refs[:-1]:
        seats = returned_ref.shape[0]

        def fill(seat, carry, returned_ref=returned_ref, first=first):
            head = order_ref[first + seat]

            @pl.when(head >= 0)
            def _():
                columns = pl.ds(pl.multiple_of(head * head_dim, head_dim), head_dim)
                out_ref[:, columns] = returned_ref[seat]

            return carry

        lax.fori_loop(0, seats, fill, 0)
        first += seats


def attend_tile(tile, width, band, data_ref, out_ref, score_ref, scale):
    stripe_len, _, rows, head_dim = data_ref.shape
    start = jnp.clip(2 * tile - band, 0, stripe_len - width)
    query = data_ref[pl.ds(2 * tile, 2), 0].reshape(2 * rows, head_dim)
    peak = None
    for chunk in range(0, width, 2):
        keys = data_ref[pl.ds(start + chunk, 2), 1].reshape(2 * rows, head_dim)
        scores = lax.dot_general(
            query, keys, (((1,), (1,)), ((), ())), preferred_element_type=jnp.float32
        )
        for part in range(2):
            key_block = start + chunk + part
            halves = []
            for half in range(2):
                outside = jnp.abs(2 * tile + half - key_block) > band
                bias = jnp.where(outside, -jnp.inf, 0.0).astype(jnp.float32)
                halves.append(
                    scores[half * rows : (half + 1) * rows, part * rows : (part + 1) * rows] + bias
                )
            masked = jnp.concatenate(halves, axis=0)
            score_ref[:, (chunk + part) * rows : (chunk + part + 1) * rows] = masked
            peak = masked if peak is None else jnp.maximum(peak, masked)
    peak = jnp.max(peak, axis=1, keepdims=True)
    total = None
    running = None
    for chunk in range(0, width, 2):
        weights = jnp.exp2(
            (score_ref[:, chunk * rows : (chunk + 2) * rows] - peak) * (scale * LOG2_E)
        )
        values = data_ref[pl.ds(start + chunk, 2), 2].reshape(2 * rows, head_dim)
        partial = weights[:, :rows] + weights[:, rows:]
        product = jnp.dot(
            weights.astype(jnp.bfloat16), values, preferred_element_type=jnp.float32
        )
        total = partial if total is None else total + partial
        running = product if running is None else running + product
    total = jnp.sum(total, axis=1, keepdims=True)
    out_ref[pl.ds(2 * tile, 2)] = (
        (running / total).astype(jnp.bfloat16).reshape(2, rows, head_dim)
    )


def attend_kernel(band_ref, data_ref, out_ref, score_ref, *, scale):
    stripe_len = data_ref.shape[0]
    band = band_ref[0]

    def step(tile, carry):
        low = jnp.maximum(2 * tile - band, 0)
        high = jnp.minimum(2 * tile + 1 + band, stripe_len - 1)
        quarter = stripe_len // 4
        level = (high - low) // quarter
        for index in range(4):

            @pl.when(level == index)
            def _():
                attend_tile(
                    tile, (index + 1) * quarter, band, data_ref, out_ref, score_ref, scale
                )

        return carry

    @pl.when(band >= 0)
    def _():
        lax.fori_loop(0, stripe_len // 2, step, 0)


def cross_kernel(query_ref, key_ref, value_ref, out_ref, *, head_dim, scale, group):
    def step(index, carry):
        for offset in range(group):
            head = index * group + offset
            columns = pl.ds(pl.multiple_of(head * head_dim, head_dim), head_dim)
            scores = lax.dot_general(
                query_ref[:, columns],
                key_ref[:, columns],
                (((1,), (1,)), ((), ())),
                preferred_element_type=jnp.float32,
            )
            peak = jnp.max(scores, axis=1, keepdims=True)
            weights = jnp.exp2((scores - peak) * (scale * LOG2_E))
            total = jnp.sum(weights, axis=1, keepdims=True)
            running = jnp.dot(
                weights.astype(jnp.bfloat16),
                value_ref[:, columns],
                preferred_element_type=jnp.float32,
            )
            out_ref[:, columns] = (running / total).astype(jnp.bfloat16)
        return carry

    lax.fori_loop(0, query_ref.shape[1] // head_dim // group, step, 0)


def narrow_kernel(place_ref, *refs, scale):
    own_refs, (low_ref, high_ref) = refs[:SEATS], refs[SEATS : SEATS + 2]
    out_refs, (query_ref, key_ref, value_ref) = refs[SEATS + 2 : -3], refs[-3:]
    per_run, _, _, _ = own_refs[0].shape
    seat, first = place_ref[0], place_ref[1]

    def step(run, carry):
        band = place_ref[2 + run]
        for turn in range(SEATS):
            there = seat ^ turn
            query_ref[there] = own_refs[turn][run, 0]
            key_ref[SEATS + there] = own_refs[turn][run, 1]
            value_ref[SEATS + there] = own_refs[turn][run, 2]
            key_ref[there] = low_ref[turn, run, 0]
            value_ref[there] = low_ref[turn, run, 1]
            key_ref[2 * SEATS + there] = high_ref[turn, run, 0]
            value_ref[2 * SEATS + there] = high_ref[turn, run, 1]

        def attend(turn):
            there = seat ^ turn
            query = query_ref[there]
            tiles = []
            for gap in range(-REACH, REACH + 1):
                scores = lax.dot_general(
                    query,
                    key_ref[SEATS + there + gap],
                    (((1,), (1,)), ((), ())),
                    preferred_element_type=jnp.float32,
                )
                if gap:
                    block = first + there + gap
                    outside = (abs(gap) > band) | (block < 0) | (block >= SB)
                    scores = scores + jnp.where(outside, -jnp.inf, 0.0).astype(jnp.float32)
                tiles.append(scores)
            peak = jnp.max(functools.reduce(jnp.maximum, tiles), axis=1, keepdims=True)
            total, running = 0.0, 0.0
            for gap, scores in enumerate(tiles, -REACH):
                weights = jnp.exp2((scores - peak) * (scale * LOG2_E))
                total = total + weights
                running = running + jnp.dot(
                    weights.astype(jnp.bfloat16),
                    value_ref[SEATS + there + gap],
                    preferred_element_type=jnp.float32,
                )
            total = jnp.sum(total, axis=1, keepdims=True)
            out_refs[turn][run] = (running / total).astype(jnp.bfloat16)

        for turn in range(SEATS):
            attend(turn)
        return carry

    lax.fori_loop(0, per_run, step, 0)


def project_kernel(context_ref, key_ref, value_ref, out_ref, total_ref):
    weights = jnp.concatenate([key_ref[...], value_ref[...]], axis=0)
    product = lax.dot_general(
        context_ref[...], weights, (((1,), (1,)), ((), ())), preferred_element_type=jnp.float32
    )

    @pl.when(pl.program_id(0) == 0)
    def _():
        total_ref[...] = product

    @pl.when(pl.program_id(0) > 0)
    def _():
        total_ref[...] += product

    @pl.when(pl.program_id(0) == pl.num_programs(0) - 1)
    def _():
        out_ref[0] = total_ref[...].astype(jnp.bfloat16)


def project(context, key_weight, value_weight, steps=4):
    text_len, depth = context.shape
    columns = key_weight.shape[1]
    part = depth // steps
    weight_spec = pl.BlockSpec((columns, part), lambda step: (0, step))
    return pl.pallas_call(
        project_kernel,
        out_shape=jax.ShapeDtypeStruct((1, text_len, 2 * columns), jnp.bfloat16),
        grid=(steps,),
        in_specs=[
            pl.BlockSpec((text_len, part), lambda step: (0, step)),
            weight_spec,
            weight_spec,
        ],
        out_specs=pl.BlockSpec((1, text_len, 2 * columns), lambda step: (0, 0, 0)),
        scratch_shapes=[pltpu.VMEM((text_len, 2 * columns), jnp.float32)],
        name="project",
    )(context, key_weight.T, value_weight.T)


def cross_pairs_kernel(
    place_ref, query_ref, mine_ref, other_ref, out_ref, key_ref, value_ref, *, head_dim, scale
):
    entries, _, pair_width = mine_ref.shape
    columns = pair_width // 2
    bits = entries.bit_length() - 1

    def attend(even_ref, odd_ref):
        def step(entry, carry):
            pair = place_ref[0]
            for bit in range(bits):
                pair = pair ^ (((entry >> bit) & 1) << (bits - 1 - bit))
            key_ref[:, :columns] = even_ref[entry, :, :columns]
            key_ref[:, columns:] = odd_ref[entry, :, :columns]
            value_ref[:, :columns] = even_ref[entry, :, columns:]
            value_ref[:, columns:] = odd_ref[entry, :, columns:]
            for offset in range(pair_width // head_dim):
                source = pl.ds(offset * head_dim, head_dim)
                target = pl.ds(
                    pl.multiple_of(pair * pair_width + offset * head_dim, head_dim), head_dim
                )
                scores = lax.dot_general(
                    query_ref[:, target],
                    key_ref[:, source],
                    (((1,), (1,)), ((), ())),
                    preferred_element_type=jnp.float32,
                )
                peak = jnp.max(scores, axis=1, keepdims=True)
                weights = jnp.exp2((scores - peak) * (scale * LOG2_E))
                total = jnp.sum(weights, axis=1, keepdims=True)
                running = jnp.dot(
                    weights.astype(jnp.bfloat16),
                    value_ref[:, source],
                    preferred_element_type=jnp.float32,
                )
                out_ref[:, target] = (running / total).astype(jnp.bfloat16)
            return carry

        lax.fori_loop(0, entries, step, 0)

    @pl.when(place_ref[1] == 0)
    def _():
        attend(mine_ref, other_ref)

    @pl.when(place_ref[1] == 1)
    def _():
        attend(other_ref, mine_ref)


def swap(values, distance):
    devices = lax.axis_size("seq")
    return lax.ppermute(values, "seq", [(source, source ^ distance) for source in range(devices)])


def doubles(key_weight, head_dim):
    devices = lax.axis_size("seq")
    return (2 * key_weight.shape[1]) % head_dim == 0 and devices & (devices - 1) == 0


def cross_attention(cross_query, context, key_weight, value_weight, head_dim, scale, text):
    devices = lax.axis_size("seq")
    device = lax.axis_index("seq")
    tok_rows, width = cross_query.shape
    out_shape = jax.ShapeDtypeStruct((tok_rows, width), jnp.bfloat16)
    vmem = pl.BlockSpec(memory_space=pltpu.VMEM)
    smem = pl.BlockSpec(memory_space=pltpu.SMEM)
    if text is None:
        text_key = jnp.dot(context, key_weight, preferred_element_type=jnp.float32)
        text_value = jnp.dot(context, value_weight, preferred_element_type=jnp.float32)
        return pl.pallas_call(
            functools.partial(cross_kernel, head_dim=head_dim, scale=scale, group=4),
            out_shape=out_shape,
            in_specs=[vmem, vmem, vmem],
            out_specs=vmem,
            name="cross",
        )(
            cross_query,
            lax.all_gather(text_key.astype(jnp.bfloat16), "seq", axis=1, tiled=True),
            lax.all_gather(text_value.astype(jnp.bfloat16), "seq", axis=1, tiled=True),
        )
    distance = devices // 4
    while distance > 1:
        came = swap(text, distance)
        text = jnp.concatenate([text, came], axis=0)
        distance //= 2
    other = swap(text, 1)
    place = jnp.stack([device // 2, device % 2]).astype(jnp.int32)
    pair = pltpu.VMEM(text.shape[1:], jnp.bfloat16)
    return pl.pallas_call(
        functools.partial(cross_pairs_kernel, head_dim=head_dim, scale=scale),
        out_shape=out_shape,
        in_specs=[smem, vmem, vmem, vmem],
        out_specs=vmem,
        scratch_shapes=[pair, pair],
        name="cross",
    )(place, cross_query, text, other)


def exchange(values):
    devices = lax.axis_size("seq")
    return lax.all_to_all(
        values,
        "seq",
        split_axis=0,
        concat_axis=0,
        tiled=True,
        axis_index_groups=[list(range(first, first + SB)) for first in range(0, devices, SB)],
    )


def attention(rank, per_run, narrow_run, arrays):
    (self_query, self_key, self_value, cross_query, context, key_weight, value_weight, band_width) = (
        arrays
    )
    devices = lax.axis_size("seq")
    device = lax.axis_index("seq")
    tok_rows, width = self_query.shape
    head_count = band_width.shape[0]
    head_dim = width // head_count
    scale = 1.0 / math.sqrt(head_dim)
    vmem = pl.BlockSpec(memory_space=pltpu.VMEM)
    smem = pl.BlockSpec(memory_space=pltpu.SMEM)
    seat = device % SEATS

    def block_array(*lead):
        return jax.ShapeDtypeStruct(lead + (tok_rows, head_dim), jnp.bfloat16)

    text = None
    if doubles(key_weight, head_dim):
        text = project(context, key_weight, value_weight)
        came = swap(text, devices // 2)
        text = jnp.concatenate([text, came], axis=0)

    slot_ids = jnp.arange(SB * per_run, dtype=jnp.int32)
    run, place = slot_ids // SB, slot_ids % SB
    wanted = run * SB + jnp.where(run % 2 == 0, place, SB - 1 - place)
    mine = jnp.where(jnp.arange(per_run) % 2 == 0, device % SB, SB - 1 - device % SB)
    mine = mine + jnp.arange(per_run, dtype=jnp.int32) * SB
    if narrow_run:
        slot_ids = jnp.arange(SEATS * narrow_run, dtype=jnp.int32)
        run, place = slot_ids % narrow_run, (slot_ids // narrow_run) ^ seat
        near = SB * per_run + run * SEATS + jnp.where(run % 2 == 0, place, SEATS - 1 - place)
        wanted = jnp.concatenate([wanted, near])
        mine = jnp.concatenate([mine, near[:narrow_run]])
    head_ids = jnp.arange(head_count, dtype=jnp.int32)
    order = jnp.sum(jnp.where(wanted[:, None] == rank[None, :], head_ids + 1, 0), axis=1) - 1
    bands = jnp.sum(jnp.where(mine[:, None] == rank[None, :], band_width + 1, 0), axis=1) - 1

    packed = pl.pallas_call(
        functools.partial(pack_kernel, head_dim=head_dim),
        out_shape=[block_array(SB, 3)] * per_run
        + [block_array(narrow_run, 3)] * (SEATS if narrow_run else 0),
        in_specs=[smem] + [vmem] * 3,
        out_specs=[vmem] * (per_run + (SEATS if narrow_run else 0)),
        name="pack",
    )(order, self_query, self_key, self_value)

    returned = []
    for index in range(per_run):
        arrived = exchange(packed[index])
        result = pl.pallas_call(
            functools.partial(attend_kernel, scale=scale),
            out_shape=block_array(SB),
            in_specs=[smem, vmem],
            out_specs=vmem,
            scratch_shapes=[pltpu.VMEM((2 * tok_rows, SB * tok_rows), jnp.float32)],
            name="attend",
        )(bands[index : index + 1], arrived)
        returned.append(exchange(result))
    if narrow_run:
        own = [packed[per_run]]
        for turn in range(1, SEATS):
            own.append(swap(packed[per_run + turn], turn))
        pairs = jnp.stack([part[:, 1:] for part in own])
        upward = [
            (source, source + SEATS)
            for source in range(devices - SEATS)
            if source // SB == (source + SEATS) // SB
        ]
        low = lax.ppermute(pairs, "seq", upward)
        high = lax.ppermute(pairs, "seq", [(high, low) for low, high in upward])
        places = jnp.stack([seat, device % SB - seat]).astype(jnp.int32)
        near = pl.pallas_call(
            functools.partial(narrow_kernel, scale=scale),
            out_shape=[block_array(narrow_run)] * SEATS,
            in_specs=[smem] + [vmem] * (SEATS + 2),
            out_specs=[vmem] * SEATS,
            scratch_shapes=[
                pltpu.VMEM((count * SEATS, tok_rows, head_dim), jnp.bfloat16)
                for count in (1, 3, 3)
            ],
            name="narrow",
        )(jnp.concatenate([places, bands[per_run:]]), *own, low, high)
        returned.append(near[0])
        for turn in range(1, SEATS):
            returned.append(swap(near[turn], turn))
    cross_out = cross_attention(
        cross_query, context, key_weight, value_weight, head_dim, scale, text
    )
    self_out = pl.pallas_call(
        functools.partial(unpack_kernel, head_dim=head_dim),
        out_shape=jax.ShapeDtypeStruct((tok_rows, width), jnp.bfloat16),
        in_specs=[smem] + [vmem] * len(returned),
        out_specs=vmem,
        name="unpack",
    )(order, *returned)
    return (self_out, cross_out)


def layer(*arrays):
    band_width = arrays[-1]
    head_count = band_width.shape[0]
    head_ids = jnp.arange(head_count, dtype=jnp.int32)
    ahead = (band_width[None, :] > band_width[:, None]) | (
        (band_width[None, :] == band_width[:, None]) & (head_ids[None, :] < head_ids[:, None])
    )
    rank = jnp.sum(ahead.astype(jnp.int32), axis=1)
    whole_run = head_count // SB
    narrow_count = head_count - whole_run * SB
    narrow_run = (narrow_count + SEATS - 1) // SEATS
    if not narrow_count or not whole_run:
        return attention(rank, (head_count + SB - 1) // SB, 0, arrays)
    close = jnp.sum((band_width <= REACH).astype(jnp.int32)) >= narrow_count
    return lax.cond(
        close,
        functools.partial(attention, rank, whole_run, narrow_run),
        functools.partial(attention, rank, whole_run + 1, 0),
        arrays,
    )


def solution(mesh):
    in_specs = (
        P(("groups", "seq"), None),
        P(("groups", "seq"), None),
        P(("groups", "seq"), None),
        P(("groups", "seq"), None),
        P("groups", None),
        P(None, "seq"),
        P(None, "seq"),
        P(),
    )
    out_specs = (P(("groups", "seq"), None), P(("groups", "seq"), None))
    return jax.shard_map(layer, mesh=mesh, in_specs=in_specs, out_specs=out_specs, check_vma=False)
```

```python
import functools
import math

import jax
import jax.numpy as jnp
from jax import lax
from jax.experimental import pallas as pl
from jax.experimental.pallas import tpu as pltpu
from jax.sharding import PartitionSpec as P


SB = 16
SEATS = 4
REACH = 4
LOG2_E = 1.4426950408889634


def pack_kernel(order_ref, query_ref, key_ref, value_ref, *out_refs, head_dim):
    sources = (query_ref, key_ref, value_ref)
    first = 0
    for out_ref in out_refs:
        seats, _ = out_ref.shape[:2]

        def fill(seat, carry, out_ref=out_ref, first=first):
            head = jnp.maximum(order_ref[first + seat], 0)
            columns = pl.ds(pl.multiple_of(head * head_dim, head_dim), head_dim)
            for index, source in enumerate(sources):
                out_ref[seat, index] = source[:, columns]
            return carry

        lax.fori_loop(0, seats, fill, 0)
        first += seats


def unpack_kernel(order_ref, *refs, head_dim):
    out_ref = refs[-1]
    first = 0
    for returned_ref in refs[:-1]:
        seats = returned_ref.shape[0]

        def fill(seat, carry, returned_ref=returned_ref, first=first):
            head = order_ref[first + seat]

            @pl.when(head >= 0)
            def _():
                columns = pl.ds(pl.multiple_of(head * head_dim, head_dim), head_dim)
                out_ref[:, columns] = returned_ref[seat]

            return carry

        lax.fori_loop(0, seats, fill, 0)
        first += seats


def attend_tile(tile, width, band, data_ref, out_ref, score_ref, scale):
    stripe_len, _, rows, head_dim = data_ref.shape
    start = jnp.clip(2 * tile - band, 0, stripe_len - width)
    query = data_ref[pl.ds(2 * tile, 2), 0].reshape(2 * rows, head_dim)
    peak = None
    for chunk in range(0, width, 2):
        keys = data_ref[pl.ds(start + chunk, 2), 1].reshape(2 * rows, head_dim)
        scores = lax.dot_general(
            query, keys, (((1,), (1,)), ((), ())), preferred_element_type=jnp.float32
        )
        for part in range(2):
            key_block = start + chunk + part
            halves = []
            for half in range(2):
                outside = jnp.abs(2 * tile + half - key_block) > band
                bias = jnp.where(outside, -jnp.inf, 0.0).astype(jnp.float32)
                halves.append(
                    scores[half * rows : (half + 1) * rows, part * rows : (part + 1) * rows] + bias
                )
            masked = jnp.concatenate(halves, axis=0)
            score_ref[:, (chunk + part) * rows : (chunk + part + 1) * rows] = masked
            peak = masked if peak is None else jnp.maximum(peak, masked)
    peak = jnp.max(peak, axis=1, keepdims=True)
    total = None
    running = None
    for chunk in range(0, width, 2):
        weights = jnp.exp2(
            (score_ref[:, chunk * rows : (chunk + 2) * rows] - peak) * (scale * LOG2_E)
        )
        values = data_ref[pl.ds(start + chunk, 2), 2].reshape(2 * rows, head_dim)
        partial = weights[:, :rows] + weights[:, rows:]
        product = jnp.dot(
            weights.astype(jnp.bfloat16), values, preferred_element_type=jnp.float32
        )
        total = partial if total is None else total + partial
        running = product if running is None else running + product
    total = jnp.sum(total, axis=1, keepdims=True)
    out_ref[pl.ds(2 * tile, 2)] = (
        (running / total).astype(jnp.bfloat16).reshape(2, rows, head_dim)
    )


def attend_kernel(band_ref, data_ref, out_ref, score_ref, *, scale):
    stripe_len = data_ref.shape[0]
    band = band_ref[0]

    def step(tile, carry):
        low = jnp.maximum(2 * tile - band, 0)
        high = jnp.minimum(2 * tile + 1 + band, stripe_len - 1)
        quarter = stripe_len // 4
        level = (high - low) // quarter
        for index in range(4):

            @pl.when(level == index)
            def _():
                attend_tile(
                    tile, (index + 1) * quarter, band, data_ref, out_ref, score_ref, scale
                )

        return carry

    @pl.when(band >= 0)
    def _():
        lax.fori_loop(0, stripe_len // 2, step, 0)


def cross_kernel(query_ref, key_ref, value_ref, out_ref, *, head_dim, scale, group):
    def step(index, carry):
        for offset in range(group):
            head = index * group + offset
            columns = pl.ds(pl.multiple_of(head * head_dim, head_dim), head_dim)
            scores = lax.dot_general(
                query_ref[:, columns],
                key_ref[:, columns],
                (((1,), (1,)), ((), ())),
                preferred_element_type=jnp.float32,
            )
            peak = jnp.max(scores, axis=1, keepdims=True)
            weights = jnp.exp2((scores - peak) * (scale * LOG2_E))
            total = jnp.sum(weights, axis=1, keepdims=True)
            running = jnp.dot(
                weights.astype(jnp.bfloat16),
                value_ref[:, columns],
                preferred_element_type=jnp.float32,
            )
            out_ref[:, columns] = (running / total).astype(jnp.bfloat16)
        return carry

    lax.fori_loop(0, query_ref.shape[1] // head_dim // group, step, 0)


def narrow_kernel(place_ref, *refs, scale):
    own_refs, (low_ref, high_ref) = refs[:SEATS], refs[SEATS : SEATS + 2]
    out_refs, (query_ref, key_ref, value_ref) = refs[SEATS + 2 : -3], refs[-3:]
    per_run, _, _, _ = own_refs[0].shape
    seat, first = place_ref[0], place_ref[1]

    def step(run, carry):
        band = place_ref[2 + run]
        for turn in range(SEATS):
            there = seat ^ turn
            query_ref[there] = own_refs[turn][run, 0]
            key_ref[SEATS + there] = own_refs[turn][run, 1]
            value_ref[SEATS + there] = own_refs[turn][run, 2]
            key_ref[there] = low_ref[turn, run, 0]
            value_ref[there] = low_ref[turn, run, 1]
            key_ref[2 * SEATS + there] = high_ref[turn, run, 0]
            value_ref[2 * SEATS + there] = high_ref[turn, run, 1]

        def attend(turn):
            there = seat ^ turn
            query = query_ref[there]
            tiles = []
            for gap in range(-REACH, REACH + 1):
                scores = lax.dot_general(
                    query,
                    key_ref[SEATS + there + gap],
                    (((1,), (1,)), ((), ())),
                    preferred_element_type=jnp.float32,
                )
                if gap:
                    block = first + there + gap
                    outside = (abs(gap) > band) | (block < 0) | (block >= SB)
                    scores = scores + jnp.where(outside, -jnp.inf, 0.0).astype(jnp.float32)
                tiles.append(scores)
            peak = jnp.max(functools.reduce(jnp.maximum, tiles), axis=1, keepdims=True)
            total, running = 0.0, 0.0
            for gap, scores in enumerate(tiles, -REACH):
                weights = jnp.exp2((scores - peak) * (scale * LOG2_E))
                total = total + weights
                running = running + jnp.dot(
                    weights.astype(jnp.bfloat16),
                    value_ref[SEATS + there + gap],
                    preferred_element_type=jnp.float32,
                )
            total = jnp.sum(total, axis=1, keepdims=True)
            out_refs[turn][run] = (running / total).astype(jnp.bfloat16)

        for turn in range(SEATS):
            attend(turn)
        return carry

    lax.fori_loop(0, per_run, step, 0)


def project_kernel(context_ref, key_ref, value_ref, out_ref, total_ref):
    weights = jnp.concatenate([key_ref[...], value_ref[...]], axis=0)
    product = lax.dot_general(
        context_ref[...], weights, (((1,), (1,)), ((), ())), preferred_element_type=jnp.float32
    )

    @pl.when(pl.program_id(0) == 0)
    def _():
        total_ref[...] = product

    @pl.when(pl.program_id(0) > 0)
    def _():
        total_ref[...] += product

    @pl.when(pl.program_id(0) == pl.num_programs(0) - 1)
    def _():
        out_ref[0] = total_ref[...].astype(jnp.bfloat16)


def project(context, key_weight, value_weight, steps=4):
    text_len, depth = context.shape
    columns = key_weight.shape[1]
    part = depth // steps
    weight_spec = pl.BlockSpec((columns, part), lambda step: (0, step))
    return pl.pallas_call(
        project_kernel,
        out_shape=jax.ShapeDtypeStruct((1, text_len, 2 * columns), jnp.bfloat16),
        grid=(steps,),
        in_specs=[
            pl.BlockSpec((text_len, part), lambda step: (0, step)),
            weight_spec,
            weight_spec,
        ],
        out_specs=pl.BlockSpec((1, text_len, 2 * columns), lambda step: (0, 0, 0)),
        scratch_shapes=[pltpu.VMEM((text_len, 2 * columns), jnp.float32)],
        name="project",
    )(context, key_weight.T, value_weight.T)


def split_kernel(place_ref, query_ref, out_ref):
    count, _, pair_width = out_ref.shape

    def fill(entry, carry):
        pair = 2 * entry + 1 - place_ref[1]
        columns = pl.ds(pl.multiple_of(pair * pair_width, pair_width), pair_width)
        out_ref[entry] = query_ref[:, columns]
        return carry

    lax.fori_loop(0, count, fill, 0)


def merge_kernel(place_ref, own_ref, came_ref, out_ref):
    count, _, pair_width = own_ref.shape

    def fill(entry, carry):
        for offset, part_ref in ((0, own_ref), (1, came_ref)):
            pair = 2 * entry + (place_ref[1] ^ offset)
            columns = pl.ds(pl.multiple_of(pair * pair_width, pair_width), pair_width)
            out_ref[:, columns] = part_ref[entry]
        return carry

    lax.fori_loop(0, count, fill, 0)


def cross_pairs_kernel(
    place_ref,
    query_ref,
    guest_ref,
    mine_ref,
    other_ref,
    own_ref,
    sent_ref,
    key_ref,
    value_ref,
    *,
    head_dim,
    scale,
):
    entries, _, pair_width = mine_ref.shape
    rows = query_ref.shape[0]
    columns = pair_width // 2
    bits = entries.bit_length() - 1

    def attend(even_ref, odd_ref):
        def step(entry, carry):
            plane = place_ref[0]
            for bit in range(bits):
                plane = plane ^ (((entry >> bit) & 1) << (bits - 1 - bit))
            key_ref[:, :columns] = even_ref[entry, :, :columns]
            key_ref[:, columns:] = odd_ref[entry, :, :columns]
            value_ref[:, :columns] = even_ref[entry, :, columns:]
            value_ref[:, columns:] = odd_ref[entry, :, columns:]
            first = (2 * plane + place_ref[1]) * pair_width
            for offset in range(pair_width // head_dim):
                source = pl.ds(offset * head_dim, head_dim)
                target = pl.ds(pl.multiple_of(first + offset * head_dim, head_dim), head_dim)
                query = jnp.concatenate(
                    [query_ref[:, target], guest_ref[plane, :, source]], axis=0
                )
                scores = lax.dot_general(
                    query,
                    key_ref[:, source],
                    (((1,), (1,)), ((), ())),
                    preferred_element_type=jnp.float32,
                )
                peak = jnp.max(scores, axis=1, keepdims=True)
                weights = jnp.exp2((scores - peak) * (scale * LOG2_E))
                total = jnp.sum(weights, axis=1, keepdims=True)
                running = jnp.dot(
                    weights.astype(jnp.bfloat16),
                    value_ref[:, source],
                    preferred_element_type=jnp.float32,
                )
                result = (running / total).astype(jnp.bfloat16)
                own_ref[plane, :, source] = result[:rows]
                sent_ref[plane, :, source] = result[rows:]
            return carry

        lax.fori_loop(0, entries, step, 0)

    @pl.when(place_ref[2] == 0)
    def _():
        attend(mine_ref, other_ref)

    @pl.when(place_ref[2] == 1)
    def _():
        attend(other_ref, mine_ref)


def swap(values, distance):
    devices = lax.axis_size("seq")
    return lax.ppermute(values, "seq", [(source, source ^ distance) for source in range(devices)])


def doubles(key_weight, head_dim):
    devices = lax.axis_size("seq")
    return (2 * key_weight.shape[1]) % head_dim == 0 and devices % 4 == 0 and devices & (devices - 1) == 0


def cross_attention(cross_query, context, key_weight, value_weight, head_dim, scale, text):
    devices = lax.axis_size("seq")
    device = lax.axis_index("seq")
    tok_rows, width = cross_query.shape
    out_shape = jax.ShapeDtypeStruct((tok_rows, width), jnp.bfloat16)
    vmem = pl.BlockSpec(memory_space=pltpu.VMEM)
    smem = pl.BlockSpec(memory_space=pltpu.SMEM)
    if text is None:
        text_key = jnp.dot(context, key_weight, preferred_element_type=jnp.float32)
        text_value = jnp.dot(context, value_weight, preferred_element_type=jnp.float32)
        return pl.pallas_call(
            functools.partial(cross_kernel, head_dim=head_dim, scale=scale, group=4),
            out_shape=out_shape,
            in_specs=[vmem, vmem, vmem],
            out_specs=vmem,
            name="cross",
        )(
            cross_query,
            lax.all_gather(text_key.astype(jnp.bfloat16), "seq", axis=1, tiled=True),
            lax.all_gather(text_value.astype(jnp.bfloat16), "seq", axis=1, tiled=True),
        )
    place = jnp.stack([device // 4, device // 2 % 2, device % 2]).astype(jnp.int32)
    pair_shape = text.shape[1:]
    part_shape = jax.ShapeDtypeStruct((devices // 4, tok_rows, pair_shape[1]), jnp.bfloat16)
    leaving = pl.pallas_call(
        split_kernel,
        out_shape=part_shape,
        in_specs=[smem, vmem],
        out_specs=vmem,
        name="split",
    )(place, cross_query)
    guests = swap(leaving, 2)
    distance = devices // 4
    while distance > 2:
        came = swap(text, distance)
        text = jnp.concatenate([text, came], axis=0)
        distance //= 2
    other = swap(text, 1)
    own, sent = pl.pallas_call(
        functools.partial(cross_pairs_kernel, head_dim=head_dim, scale=scale),
        out_shape=[part_shape] * 2,
        in_specs=[smem] + [vmem] * 4,
        out_specs=[vmem] * 2,
        scratch_shapes=[pltpu.VMEM(pair_shape, jnp.bfloat16)] * 2,
        name="cross",
    )(place, cross_query, guests, text, other)
    back = swap(sent, 2)
    return pl.pallas_call(
        merge_kernel,
        out_shape=out_shape,
        in_specs=[smem, vmem, vmem],
        out_specs=vmem,
        name="merge",
    )(place, own, back)


def exchange(values):
    devices = lax.axis_size("seq")
    return lax.all_to_all(
        values,
        "seq",
        split_axis=0,
        concat_axis=0,
        tiled=True,
        axis_index_groups=[list(range(first, first + SB)) for first in range(0, devices, SB)],
    )


def pack(order, sources, shapes, head_dim):
    vmem = pl.BlockSpec(memory_space=pltpu.VMEM)
    return pl.pallas_call(
        functools.partial(pack_kernel, head_dim=head_dim),
        out_shape=shapes,
        in_specs=[pl.BlockSpec(memory_space=pltpu.SMEM)] + [vmem] * 3,
        out_specs=[vmem] * len(shapes),
        name="pack",
    )(order, *sources)


def run_slot(outgoing, band, scale):
    stripe_len, _, tok_rows, head_dim = outgoing.shape
    vmem = pl.BlockSpec(memory_space=pltpu.VMEM)
    arrived = exchange(outgoing)
    result = pl.pallas_call(
        functools.partial(attend_kernel, scale=scale),
        out_shape=jax.ShapeDtypeStruct((stripe_len, tok_rows, head_dim), jnp.bfloat16),
        in_specs=[pl.BlockSpec(memory_space=pltpu.SMEM), vmem],
        out_specs=vmem,
        scratch_shapes=[pltpu.VMEM((2 * tok_rows, stripe_len * tok_rows), jnp.float32)],
        name="attend",
    )(band, arrived)
    return exchange(result)


def layer(
    self_query, self_key, self_value, cross_query, context, key_weight, value_weight, band_width
):
    devices = lax.axis_size("seq")
    device = lax.axis_index("seq")
    tok_rows, width = self_query.shape
    head_count = band_width.shape[0]
    head_dim = width // head_count
    scale = 1.0 / math.sqrt(head_dim)
    vmem = pl.BlockSpec(memory_space=pltpu.VMEM)
    smem = pl.BlockSpec(memory_space=pltpu.SMEM)
    seat, turn_seat = device % SEATS, device % SB
    sources = (self_query, self_key, self_value)

    def block_array(*lead):
        return jax.ShapeDtypeStruct(lead + (tok_rows, head_dim), jnp.bfloat16)

    text = None
    if doubles(key_weight, head_dim):
        text = project(context, key_weight, value_weight)
        came = swap(text, devices // 2)
        text = jnp.concatenate([text, came], axis=0)

    whole_run = head_count // SB
    rest = head_count - whole_run * SB
    narrow_run = (rest + SEATS - 1) // SEATS
    head_ids = jnp.arange(head_count, dtype=jnp.int32)
    ahead = (band_width[None, :] > band_width[:, None]) | (
        (band_width[None, :] == band_width[:, None]) & (head_ids[None, :] < head_ids[:, None])
    )
    rank = jnp.sum(ahead.astype(jnp.int32), axis=1)
    close = jnp.sum((band_width <= REACH).astype(jnp.int32)) >= rest
    slot_ids = jnp.arange(SB * (whole_run + 1), dtype=jnp.int32)
    run, place = slot_ids // SB, slot_ids % SB
    wanted = run * SB + jnp.where(run % 2 == 0, place, SB - 1 - place)
    runs = jnp.arange(whole_run + 1, dtype=jnp.int32)
    mine = runs * SB + jnp.where(runs % 2 == 0, turn_seat, SB - 1 - turn_seat)
    slot_ids = jnp.arange(SEATS * narrow_run, dtype=jnp.int32)
    run, place = slot_ids % narrow_run, (slot_ids // narrow_run) ^ seat
    near = SB * whole_run + run * SEATS + jnp.where(run % 2 == 0, place, SEATS - 1 - place)
    wanted = jnp.concatenate([wanted, near])
    mine = jnp.concatenate([mine, near[:narrow_run]])
    order = jnp.sum(jnp.where(wanted[:, None] == rank[None, :], head_ids + 1, 0), axis=1) - 1
    bands = jnp.sum(jnp.where(mine[:, None] == rank[None, :], band_width + 1, 0), axis=1) - 1
    wide_slots, last_slots = SB * whole_run, SB * (whole_run + 1)

    shapes = [block_array(SB, 3)] * whole_run + [block_array(narrow_run, 3)] * SEATS
    packed = pack(
        jnp.concatenate([order[:wide_slots], order[last_slots:]]), sources, shapes, head_dim
    )
    returned = [
        run_slot(packed[index], bands[index : index + 1], scale)
        for index in range(whole_run)
    ]
    own = [packed[whole_run]]
    for turn in range(1, SEATS):
        own.append(swap(packed[whole_run + turn], turn))
    pairs = jnp.stack([part[:, 1:] for part in own])
    upward = [
        (source, source + SEATS)
        for source in range(devices - SEATS)
        if source // SB == (source + SEATS) // SB
    ]
    low = lax.ppermute(pairs, "seq", upward)
    high = lax.ppermute(pairs, "seq", [(high, low) for low, high in upward])
    places = jnp.stack([seat, turn_seat - seat]).astype(jnp.int32)
    near_out = pl.pallas_call(
        functools.partial(narrow_kernel, scale=scale),
        out_shape=[block_array(narrow_run)] * SEATS,
        in_specs=[smem] + [vmem] * (SEATS + 2),
        out_specs=[vmem] * SEATS,
        scratch_shapes=[
            pltpu.VMEM((count * SEATS, tok_rows, head_dim), jnp.bfloat16)
            for count in (1, 3, 3)
        ],
        name="narrow",
    )(jnp.concatenate([places, bands[whole_run + 1 :]]), *own, low, high)
    nears = [near_out[0]]
    for turn in range(1, SEATS):
        nears.append(swap(near_out[turn], turn))
    cross_out = cross_attention(
        cross_query, context, key_weight, value_weight, head_dim, scale, text
    )

    def unpack(order, parts):
        return pl.pallas_call(
            functools.partial(unpack_kernel, head_dim=head_dim),
            out_shape=jax.ShapeDtypeStruct((tok_rows, width), jnp.bfloat16),
            in_specs=[smem] + [vmem] * len(parts),
            out_specs=vmem,
            name="unpack",
        )(order, *parts)

    wide_order, rest_order = order[:wide_slots], order[wide_slots:last_slots]
    near_order = order[last_slots:]

    def short(operands):
        parts, nears, _ = operands
        return unpack(jnp.concatenate([wide_order, near_order]), [*parts, *nears])

    def full(operands):
        parts, _, sources = operands
        (outgoing,) = pack(rest_order, sources, [block_array(SB, 3)], head_dim)
        last = run_slot(outgoing, bands[whole_run : whole_run + 1], scale)
        return unpack(jnp.concatenate([wide_order, rest_order]), [*parts, last])

    self_out = lax.cond(close, short, full, (returned, nears, sources))
    return (self_out, cross_out)


def solution(mesh):
    in_specs = (
        P(("groups", "seq"), None),
        P(("groups", "seq"), None),
        P(("groups", "seq"), None),
        P(("groups", "seq"), None),
        P("groups", None),
        P(None, "seq"),
        P(None, "seq"),
        P(),
    )
    out_specs = (P(("groups", "seq"), None), P(("groups", "seq"), None))
    return jax.shard_map(layer, mesh=mesh, in_specs=in_specs, out_specs=out_specs, check_vma=False)
```

```python
import functools
import math

import jax
import jax.numpy as jnp
from jax import lax
from jax.experimental import pallas as pl
from jax.experimental.pallas import tpu as pltpu
from jax.sharding import PartitionSpec as P


SB = 16
SEATS = 4
REACH = 4
ROOM = pltpu.CompilerParams(vmem_limit_bytes=24 << 20)
LOG2_E = 1.4426950408889634


def pack_kernel(order_ref, query_ref, key_ref, value_ref, *out_refs, head_dim):
    sources = (query_ref, key_ref, value_ref)
    first = 0
    for out_ref in out_refs:
        seats, _ = out_ref.shape[:2]

        def fill(seat, carry, out_ref=out_ref, first=first):
            head = jnp.maximum(order_ref[first + seat], 0)
            columns = pl.ds(pl.multiple_of(head * head_dim, head_dim), head_dim)
            for index, source in enumerate(sources):
                out_ref[seat, index] = source[:, columns]
            return carry

        lax.fori_loop(0, seats, fill, 0)
        first += seats


def unpack_kernel(order_ref, *refs, head_dim):
    out_ref, done = refs[-2:]
    first = 0
    for returned_ref in refs[:-2]:
        seats, runs = returned_ref.shape[:2]
        for run in range(runs):

            def fill(seat, carry, returned_ref=returned_ref, first=first, run=run):
                head = order_ref[first + seat]

                @pl.when(head >= 0)
                def _():
                    columns = pl.ds(pl.multiple_of(head * head_dim, head_dim), head_dim)
                    pltpu.make_async_copy(
                        returned_ref.at[seat, run], out_ref.at[:, columns], done
                    ).start()

                return carry

            lax.fori_loop(0, seats, fill, 0)
            first += seats
    pltpu.make_async_copy(out_ref, out_ref, done).wait()


def attend_tile(tile, width, band, data_ref, out_ref, score_ref, scale):
    stripe_len, _, rows, head_dim = data_ref.shape
    start = jnp.clip(2 * tile - band, 0, stripe_len - width)
    query = data_ref[pl.ds(2 * tile, 2), 0].reshape(2 * rows, head_dim)
    peak = None
    for chunk in range(0, width, 2):
        keys = data_ref[pl.ds(start + chunk, 2), 1].reshape(2 * rows, head_dim)
        scores = lax.dot_general(
            query, keys, (((1,), (1,)), ((), ())), preferred_element_type=jnp.float32
        )
        for part in range(2):
            key_block = start + chunk + part
            halves = []
            for half in range(2):
                outside = jnp.abs(2 * tile + half - key_block) > band
                bias = jnp.where(outside, -jnp.inf, 0.0).astype(jnp.float32)
                halves.append(
                    scores[half * rows : (half + 1) * rows, part * rows : (part + 1) * rows] + bias
                )
            masked = jnp.concatenate(halves, axis=0)
            score_ref[:, (chunk + part) * rows : (chunk + part + 1) * rows] = masked
            peak = masked if peak is None else jnp.maximum(peak, masked)
    peak = jnp.max(peak, axis=1, keepdims=True)
    total = None
    running = None
    for chunk in range(0, width, 2):
        weights = jnp.exp2(
            (score_ref[:, chunk * rows : (chunk + 2) * rows] - peak) * (scale * LOG2_E)
        )
        values = data_ref[pl.ds(start + chunk, 2), 2].reshape(2 * rows, head_dim)
        partial = weights[:, :rows] + weights[:, rows:]
        product = jnp.dot(
            weights.astype(jnp.bfloat16), values, preferred_element_type=jnp.float32
        )
        total = partial if total is None else total + partial
        running = product if running is None else running + product
    total = jnp.sum(total, axis=1, keepdims=True)
    out_ref[pl.ds(2 * tile, 2), 0] = (
        (running / total).astype(jnp.bfloat16).reshape(2, rows, head_dim)
    )


def attend_kernel(band_ref, source_ref, *refs, scale):
    out_ref, score_ref, data_ref, done = refs[-4:]
    load = pltpu.make_async_copy(source_ref, data_ref, done)
    load.start()
    load.wait()
    stripe_len = data_ref.shape[0]
    band = band_ref[0]

    def step(tile, carry):
        low = jnp.maximum(2 * tile - band, 0)
        high = jnp.minimum(2 * tile + 1 + band, stripe_len - 1)
        quarter = stripe_len // 4
        level = (high - low) // quarter
        for index in range(4):

            @pl.when(level == index)
            def _():
                attend_tile(
                    tile, (index + 1) * quarter, band, data_ref, out_ref, score_ref, scale
                )

        return carry

    @pl.when(band >= 0)
    def _():
        lax.fori_loop(0, stripe_len // 2, step, 0)


def cross_kernel(query_ref, key_ref, value_ref, out_ref, *, head_dim, scale, group):
    def step(index, carry):
        for offset in range(group):
            head = index * group + offset
            columns = pl.ds(pl.multiple_of(head * head_dim, head_dim), head_dim)
            scores = lax.dot_general(
                query_ref[:, columns],
                key_ref[:, columns],
                (((1,), (1,)), ((), ())),
                preferred_element_type=jnp.float32,
            )
            peak = jnp.max(scores, axis=1, keepdims=True)
            weights = jnp.exp2((scores - peak) * (scale * LOG2_E))
            total = jnp.sum(weights, axis=1, keepdims=True)
            running = jnp.dot(
                weights.astype(jnp.bfloat16),
                value_ref[:, columns],
                preferred_element_type=jnp.float32,
            )
            out_ref[:, columns] = (running / total).astype(jnp.bfloat16)
        return carry

    lax.fori_loop(0, query_ref.shape[1] // head_dim // group, step, 0)


def pairs_kernel(*refs):
    for turn, own_ref in enumerate(refs[:-1]):
        refs[-1][turn] = own_ref[:, 1:]


def narrow_kernel(place_ref, *refs, scale):
    own_refs, (low_ref, high_ref) = refs[:SEATS], refs[SEATS : SEATS + 2]
    out_refs, (query_ref, key_ref, value_ref) = refs[SEATS + 2 : -3], refs[-3:]
    per_run, _, _, _ = own_refs[0].shape
    seat, first = place_ref[0], place_ref[1]

    def step(run, carry):
        band = place_ref[2 + run]
        for turn in range(SEATS):
            there = seat ^ turn
            query_ref[there] = own_refs[turn][run, 0]
            key_ref[SEATS + there] = own_refs[turn][run, 1]
            value_ref[SEATS + there] = own_refs[turn][run, 2]
            key_ref[there] = low_ref[turn, run, 0]
            value_ref[there] = low_ref[turn, run, 1]
            key_ref[2 * SEATS + there] = high_ref[turn, run, 0]
            value_ref[2 * SEATS + there] = high_ref[turn, run, 1]

        def attend(turn):
            there = seat ^ turn
            query = query_ref[there]
            tiles = []
            for gap in range(-REACH, REACH + 1):
                scores = lax.dot_general(
                    query,
                    key_ref[SEATS + there + gap],
                    (((1,), (1,)), ((), ())),
                    preferred_element_type=jnp.float32,
                )
                if gap:
                    block = first + there + gap
                    outside = (abs(gap) > band) | (block < 0) | (block >= SB)
                    scores = scores + jnp.where(outside, -jnp.inf, 0.0).astype(jnp.float32)
                tiles.append(scores)
            peak = jnp.max(functools.reduce(jnp.maximum, tiles), axis=1, keepdims=True)
            total, running = 0.0, 0.0
            for gap, scores in enumerate(tiles, -REACH):
                weights = jnp.exp2((scores - peak) * (scale * LOG2_E))
                total = total + weights
                running = running + jnp.dot(
                    weights.astype(jnp.bfloat16),
                    value_ref[SEATS + there + gap],
                    preferred_element_type=jnp.float32,
                )
            total = jnp.sum(total, axis=1, keepdims=True)
            out_refs[turn][run] = (running / total).astype(jnp.bfloat16)

        for turn in range(SEATS):
            attend(turn)
        return carry

    lax.fori_loop(0, per_run, step, 0)


def project_kernel(context_ref, key_ref, value_ref, out_ref, total_ref):
    weights = jnp.concatenate([key_ref[...], value_ref[...]], axis=0)
    product = lax.dot_general(
        context_ref[...], weights, (((1,), (1,)), ((), ())), preferred_element_type=jnp.float32
    )

    @pl.when(pl.program_id(0) == 0)
    def _():
        total_ref[...] = product

    @pl.when(pl.program_id(0) > 0)
    def _():
        total_ref[...] += product

    @pl.when(pl.program_id(0) == pl.num_programs(0) - 1)
    def _():
        out_ref[0] = total_ref[...].astype(jnp.bfloat16)


def project(context, key_weight, value_weight, steps=2):
    text_len, depth = context.shape
    columns = key_weight.shape[1]
    part = depth // steps
    weight_spec = pl.BlockSpec((columns, part), lambda step: (0, step))
    return pl.pallas_call(
        project_kernel,
        out_shape=jax.ShapeDtypeStruct((1, text_len, 2 * columns), jnp.bfloat16),
        grid=(steps,),
        in_specs=[
            pl.BlockSpec((text_len, part), lambda step: (0, step)),
            weight_spec,
            weight_spec,
        ],
        out_specs=pl.BlockSpec((1, text_len, 2 * columns), lambda step: (0, 0, 0)),
        scratch_shapes=[pltpu.VMEM((text_len, 2 * columns), jnp.float32)],
        name="project",
    )(context, key_weight.T, value_weight.T)


def split_kernel(place_ref, query_ref, out_ref):
    count, _, pair_width = out_ref.shape

    def fill(entry, carry):
        pair = 2 * entry + 1 - place_ref[1]
        columns = pl.ds(pl.multiple_of(pair * pair_width, pair_width), pair_width)
        out_ref[entry] = query_ref[:, columns]
        return carry

    lax.fori_loop(0, count, fill, 0)


def merge_kernel(place_ref, own_ref, came_ref, out_ref):
    count, _, pair_width = own_ref.shape

    def fill(entry, carry):
        for offset, part_ref in ((0, own_ref), (1, came_ref)):
            pair = 2 * entry + (place_ref[1] ^ offset)
            columns = pl.ds(pl.multiple_of(pair * pair_width, pair_width), pair_width)
            out_ref[:, columns] = part_ref[entry]
        return carry

    lax.fori_loop(0, count, fill, 0)


def cross_pairs_kernel(
    place_ref,
    query_ref,
    guest_ref,
    mine_ref,
    other_ref,
    own_ref,
    sent_ref,
    key_ref,
    value_ref,
    *,
    head_dim,
    scale,
):
    entries, _, pair_width = mine_ref.shape
    rows = query_ref.shape[0]
    columns = pair_width // 2
    bits = entries.bit_length() - 1

    def attend(even_ref, odd_ref):
        def step(entry, carry):
            plane = place_ref[0]
            for bit in range(bits):
                plane = plane ^ (((entry >> bit) & 1) << (bits - 1 - bit))
            key_ref[:, :columns] = even_ref[entry, :, :columns]
            key_ref[:, columns:] = odd_ref[entry, :, :columns]
            value_ref[:, :columns] = even_ref[entry, :, columns:]
            value_ref[:, columns:] = odd_ref[entry, :, columns:]
            first = (2 * plane + place_ref[1]) * pair_width
            for offset in range(pair_width // head_dim):
                source = pl.ds(offset * head_dim, head_dim)
                target = pl.ds(pl.multiple_of(first + offset * head_dim, head_dim), head_dim)
                query = jnp.concatenate(
                    [query_ref[:, target], guest_ref[plane, :, source]], axis=0
                )
                scores = lax.dot_general(
                    query,
                    key_ref[:, source],
                    (((1,), (1,)), ((), ())),
                    preferred_element_type=jnp.float32,
                )
                peak = jnp.max(scores, axis=1, keepdims=True)
                weights = jnp.exp2((scores - peak) * (scale * LOG2_E))
                total = jnp.sum(weights, axis=1, keepdims=True)
                running = jnp.dot(
                    weights.astype(jnp.bfloat16),
                    value_ref[:, source],
                    preferred_element_type=jnp.float32,
                )
                result = (running / total).astype(jnp.bfloat16)
                own_ref[plane, :, source] = result[:rows]
                sent_ref[plane, :, source] = result[rows:]
            return carry

        lax.fori_loop(0, entries, step, 0)

    @pl.when(place_ref[2] == 0)
    def _():
        attend(mine_ref, other_ref)

    @pl.when(place_ref[2] == 1)
    def _():
        attend(other_ref, mine_ref)


def swap(values, distance):
    devices = lax.axis_size("seq")
    return lax.ppermute(values, "seq", [(source, source ^ distance) for source in range(devices)])


def doubles(key_weight, head_dim):
    devices = lax.axis_size("seq")
    return (2 * key_weight.shape[1]) % head_dim == 0 and devices % 4 == 0 and devices & (devices - 1) == 0


def cross_attention(cross_query, context, key_weight, value_weight, head_dim, scale, text):
    devices = lax.axis_size("seq")
    device = lax.axis_index("seq")
    tok_rows, width = cross_query.shape
    out_shape = jax.ShapeDtypeStruct((tok_rows, width), jnp.bfloat16)
    vmem = pl.BlockSpec(memory_space=pltpu.VMEM)
    smem = pl.BlockSpec(memory_space=pltpu.SMEM)
    if text is None:
        text_key = jnp.dot(context, key_weight, preferred_element_type=jnp.float32)
        text_value = jnp.dot(context, value_weight, preferred_element_type=jnp.float32)
        return pl.pallas_call(
            functools.partial(cross_kernel, head_dim=head_dim, scale=scale, group=4),
            out_shape=out_shape,
            in_specs=[vmem, vmem, vmem],
            out_specs=vmem,
            name="cross",
            compiler_params=ROOM,
        )(
            cross_query,
            lax.all_gather(text_key.astype(jnp.bfloat16), "seq", axis=1, tiled=True),
            lax.all_gather(text_value.astype(jnp.bfloat16), "seq", axis=1, tiled=True),
        )
    place = jnp.stack([device // 4, device // 2 % 2, device % 2]).astype(jnp.int32)
    pair_shape = text.shape[1:]
    part_shape = jax.ShapeDtypeStruct((devices // 4, tok_rows, pair_shape[1]), jnp.bfloat16)
    leaving = pl.pallas_call(
        split_kernel,
        out_shape=part_shape,
        in_specs=[smem, vmem],
        out_specs=vmem,
        name="split",
        compiler_params=ROOM,
    )(place, cross_query)
    guests = swap(leaving, 2)
    distance = devices // 4
    while distance > 2:
        came = swap(text, distance)
        text = jnp.concatenate([text, came], axis=0)
        distance //= 2
    other = swap(text, 1)
    own, sent = pl.pallas_call(
        functools.partial(cross_pairs_kernel, head_dim=head_dim, scale=scale),
        out_shape=[part_shape] * 2,
        in_specs=[smem] + [vmem] * 4,
        out_specs=[vmem] * 2,
        scratch_shapes=[pltpu.VMEM(pair_shape, jnp.bfloat16)] * 2,
        name="cross",
        compiler_params=ROOM,
    )(place, cross_query, guests, text, other)
    back = swap(sent, 2)
    return pl.pallas_call(
        merge_kernel,
        out_shape=out_shape,
        in_specs=[smem, vmem, vmem],
        out_specs=vmem,
        name="merge",
        compiler_params=ROOM,
    )(place, own, back)


def exchange(values):
    devices = lax.axis_size("seq")
    return lax.all_to_all(
        values,
        "seq",
        split_axis=0,
        concat_axis=0,
        tiled=True,
        axis_index_groups=[list(range(first, first + SB)) for first in range(0, devices, SB)],
    )


def pack(order, sources, shapes, head_dim):
    vmem = pl.BlockSpec(memory_space=pltpu.VMEM)
    return pl.pallas_call(
        functools.partial(pack_kernel, head_dim=head_dim),
        out_shape=shapes,
        in_specs=[pl.BlockSpec(memory_space=pltpu.SMEM)] + [vmem] * 3,
        out_specs=[vmem] * len(shapes),
        name="pack",
    )(order, *sources)


def run_slots(outgoing, bands, scale):
    stripe_len, _, tok_rows, head_dim = outgoing[0].shape
    result = None
    for index, values in enumerate(outgoing):
        arrived = exchange(values)
        result = pl.pallas_call(
            functools.partial(attend_kernel, scale=scale),
            out_shape=jax.ShapeDtypeStruct(
                (stripe_len, len(outgoing), tok_rows, head_dim), jnp.bfloat16
            ),
            grid=(1,),
            in_specs=[
                pl.BlockSpec(memory_space=pltpu.SMEM),
                pl.BlockSpec(memory_space=pl.ANY),
            ]
            + ([] if result is None else [pl.BlockSpec(memory_space=pl.ANY)]),
            out_specs=pl.BlockSpec(
                (stripe_len, 1, tok_rows, head_dim),
                lambda step, index=index: (0, index, 0, 0),
            ),
            scratch_shapes=[
                pltpu.VMEM((2 * tok_rows, stripe_len * tok_rows), jnp.float32),
                pltpu.VMEM(values.shape, jnp.bfloat16),
                pltpu.SemaphoreType.DMA,
            ],
            input_output_aliases={} if result is None else {2: 0},
            compiler_params=ROOM,
            name="attend",
        )(bands[index : index + 1], arrived, *([] if result is None else [result]))
    return exchange(result)


def layer(
    self_query, self_key, self_value, cross_query, context, key_weight, value_weight, band_width
):
    devices = lax.axis_size("seq")
    device = lax.axis_index("seq")
    tok_rows, width = self_query.shape
    head_count = band_width.shape[0]
    head_dim = width // head_count
    scale = 1.0 / math.sqrt(head_dim)
    vmem = pl.BlockSpec(memory_space=pltpu.VMEM)
    smem = pl.BlockSpec(memory_space=pltpu.SMEM)
    seat, turn_seat = device % SEATS, device % SB
    sources = (self_query, self_key, self_value)

    def block_array(*lead):
        return jax.ShapeDtypeStruct(lead + (tok_rows, head_dim), jnp.bfloat16)

    text = None
    if doubles(key_weight, head_dim):
        text = project(context, key_weight, value_weight)
        came = swap(text, devices // 2)
        text = jnp.concatenate([text, came], axis=0)

    whole_run = head_count // SB
    rest = head_count - whole_run * SB
    narrow_run = (rest + SEATS - 1) // SEATS
    head_ids = jnp.arange(head_count, dtype=jnp.int32)
    ahead = (band_width[None, :] > band_width[:, None]) | (
        (band_width[None, :] == band_width[:, None]) & (head_ids[None, :] < head_ids[:, None])
    )
    rank = jnp.sum(ahead.astype(jnp.int32), axis=1)
    close = jnp.sum((band_width <= REACH).astype(jnp.int32)) >= rest
    slot_ids = jnp.arange(SB * (whole_run + 1), dtype=jnp.int32)
    run, place = slot_ids // SB, slot_ids % SB
    wanted = run * SB + jnp.where(run % 2 == 0, place, SB - 1 - place)
    runs = jnp.arange(whole_run + 1, dtype=jnp.int32)
    mine = runs * SB + jnp.where(runs % 2 == 0, turn_seat, SB - 1 - turn_seat)
    slot_ids = jnp.arange(SEATS * narrow_run, dtype=jnp.int32)
    run, place = slot_ids % narrow_run, (slot_ids // narrow_run) ^ seat
    near = SB * whole_run + run * SEATS + jnp.where(run % 2 == 0, place, SEATS - 1 - place)
    wanted = jnp.concatenate([wanted, near])
    mine = jnp.concatenate([mine, near[:narrow_run]])
    order = jnp.sum(jnp.where(wanted[:, None] == rank[None, :], head_ids + 1, 0), axis=1) - 1
    bands = jnp.sum(jnp.where(mine[:, None] == rank[None, :], band_width + 1, 0), axis=1) - 1
    wide_slots, last_slots = SB * whole_run, SB * (whole_run + 1)

    shapes = [block_array(SB, 3)] * whole_run + [block_array(narrow_run, 3)] * SEATS
    packed = pack(
        jnp.concatenate([order[:wide_slots], order[last_slots:]]), sources, shapes, head_dim
    )
    returned = run_slots(packed[:whole_run], bands[:whole_run], scale)
    own = [packed[whole_run]]
    for turn in range(1, SEATS):
        own.append(swap(packed[whole_run + turn], turn))
    pairs = pl.pallas_call(
        pairs_kernel,
        out_shape=block_array(SEATS, narrow_run, 2),
        in_specs=[vmem] * SEATS,
        out_specs=vmem,
        name="pairs",
    )(*own)
    upward = [
        (source, source + SEATS)
        for source in range(devices - SEATS)
        if source // SB == (source + SEATS) // SB
    ]
    low = lax.ppermute(pairs, "seq", upward)
    high = lax.ppermute(pairs, "seq", [(high, low) for low, high in upward])
    places = jnp.stack([seat, turn_seat - seat]).astype(jnp.int32)
    near_out = pl.pallas_call(
        functools.partial(narrow_kernel, scale=scale),
        out_shape=[block_array(narrow_run)] * SEATS,
        in_specs=[smem] + [vmem] * (SEATS + 2),
        out_specs=[vmem] * SEATS,
        scratch_shapes=[
            pltpu.VMEM((count * SEATS, tok_rows, head_dim), jnp.bfloat16)
            for count in (1, 3, 3)
        ],
        name="narrow",
        compiler_params=ROOM,
    )(jnp.concatenate([places, bands[whole_run + 1 :]]), *own, low, high)
    nears = [near_out[0]]
    for turn in range(1, SEATS):
        nears.append(swap(near_out[turn], turn))
    cross_out = cross_attention(
        cross_query, context, key_weight, value_weight, head_dim, scale, text
    )

    def full(sources):
        (outgoing,) = pack(
            order[wide_slots:last_slots], sources, [block_array(SB, 3)], head_dim
        )
        return run_slots([outgoing], bands[whole_run : whole_run + 1], scale)

    def short(sources):
        return jnp.zeros((SB, 1, tok_rows, head_dim), jnp.bfloat16)

    last = lax.cond(close, short, full, sources)
    slot_ids = jnp.arange(order.shape[0], dtype=jnp.int32)
    from_last = (slot_ids >= wide_slots) & (slot_ids < last_slots)
    unused = jnp.where(close, from_last, slot_ids >= last_slots)
    parts = [returned, last] + [part[:, None] for part in nears]
    self_out = pl.pallas_call(
        functools.partial(unpack_kernel, head_dim=head_dim),
        out_shape=jax.ShapeDtypeStruct((tok_rows, width), jnp.bfloat16),
        in_specs=[smem] + [vmem] * len(parts),
        out_specs=pl.BlockSpec(memory_space=pl.ANY),
        scratch_shapes=[pltpu.SemaphoreType.DMA],
        name="unpack",
        compiler_params=ROOM,
    )(jnp.where(unused, -1, order), *parts)
    return (self_out, cross_out)


def solution(mesh):
    in_specs = (
        P(("groups", "seq"), None),
        P(("groups", "seq"), None),
        P(("groups", "seq"), None),
        P(("groups", "seq"), None),
        P("groups", None),
        P(None, "seq"),
        P(None, "seq"),
        P(),
    )
    out_specs = (P(("groups", "seq"), None), P(("groups", "seq"), None))
    return jax.shard_map(layer, mesh=mesh, in_specs=in_specs, out_specs=out_specs, check_vma=False)
```

```python
import functools
import math

import jax
import jax.numpy as jnp
from jax import lax
from jax.experimental import pallas as pl
from jax.experimental.pallas import tpu as pltpu
from jax.sharding import PartitionSpec as P


SB = 16
SEATS = 4
REACH = 4
ROOM = pltpu.CompilerParams(vmem_limit_bytes=24 << 20)
LOG2_E = 1.4426950408889634


def pack_kernel(order_ref, query_ref, key_ref, value_ref, *out_refs, head_dim):
    sources = (query_ref, key_ref, value_ref)
    first = 0
    for out_ref in out_refs:
        seats, _ = out_ref.shape[:2]

        def fill(seat, carry, out_ref=out_ref, first=first):
            head = jnp.maximum(order_ref[first + seat], 0)
            columns = pl.ds(pl.multiple_of(head * head_dim, head_dim), head_dim)
            for index, source in enumerate(sources):
                out_ref[seat, index] = source[:, columns]
            return carry

        lax.fori_loop(0, seats, fill, 0)
        first += seats


def unpack_kernel(order_ref, *refs, head_dim):
    out_ref, done = refs[-2:]
    first = 0
    for returned_ref in refs[:-2]:
        seats, runs = returned_ref.shape[:2]
        for run in range(runs):

            def fill(seat, carry, returned_ref=returned_ref, first=first, run=run):
                head = order_ref[first + seat]

                @pl.when(head >= 0)
                def _():
                    columns = pl.ds(pl.multiple_of(head * head_dim, head_dim), head_dim)
                    pltpu.make_async_copy(
                        returned_ref.at[seat, run], out_ref.at[:, columns], done
                    ).start()

                return carry

            lax.fori_loop(0, seats, fill, 0)
            first += seats
    pltpu.make_async_copy(out_ref, out_ref, done).wait()


def score_step(tile, chunk, width, band, data_ref, score_ref, peak):
    stripe_len, _, rows, head_dim = data_ref.shape
    start = jnp.clip(2 * tile - band, 0, stripe_len - width)
    query = data_ref[pl.ds(2 * tile, 2), 0].reshape(2 * rows, head_dim)
    keys = data_ref[pl.ds(start + chunk, 2), 1].reshape(2 * rows, head_dim)
    scores = lax.dot_general(
        query, keys, (((1,), (1,)), ((), ())), preferred_element_type=jnp.float32
    )
    for part in range(2):
        key_block = start + chunk + part
        halves = []
        for half in range(2):
            outside = jnp.abs(2 * tile + half - key_block) > band
            bias = jnp.where(outside, -jnp.inf, 0.0).astype(jnp.float32)
            halves.append(
                scores[half * rows : (half + 1) * rows, part * rows : (part + 1) * rows] + bias
            )
        masked = jnp.concatenate(halves, axis=0)
        score_ref[:, (chunk + part) * rows : (chunk + part + 1) * rows] = masked
        peak = masked if peak is None else jnp.maximum(peak, masked)
    return peak


def value_step(tile, chunk, width, band, data_ref, score_ref, peak, totals, scale):
    stripe_len, _, rows, head_dim = data_ref.shape
    start = jnp.clip(2 * tile - band, 0, stripe_len - width)
    weights = jnp.exp2(
        (score_ref[:, chunk * rows : (chunk + 2) * rows] - peak) * (scale * LOG2_E)
    )
    values = data_ref[pl.ds(start + chunk, 2), 2].reshape(2 * rows, head_dim)
    partial = weights[:, :rows] + weights[:, rows:]
    product = jnp.dot(weights.astype(jnp.bfloat16), values, preferred_element_type=jnp.float32)
    if totals is None:
        return partial, product
    return totals[0] + partial, totals[1] + product


def attend_width(width, band, data_ref, out_ref, score_refs, peak_refs, scale, late):
    stripe_len, _, rows, head_dim = data_ref.shape
    tiles = stripe_len // 2
    peak = None
    for chunk in range(0, width, 2):
        peak = score_step(0, chunk, width, band, data_ref, score_refs[0], peak)
    peak_refs[0][...] = peak
    late.wait()

    def step(pair, carry):
        for turn in range(2):
            tile = 2 * pair + turn
            following = jnp.minimum(tile + 1, tiles - 1)
            peak = jnp.max(peak_refs[turn][...], axis=1, keepdims=True)
            ahead, totals = None, None
            for chunk in range(0, width, 2):
                ahead = score_step(
                    following, chunk, width, band, data_ref, score_refs[1 - turn], ahead
                )
                totals = value_step(
                    tile, chunk, width, band, data_ref, score_refs[turn], peak, totals, scale
                )
            peak_refs[1 - turn][...] = ahead
            total = jnp.sum(totals[0], axis=1, keepdims=True)
            out_ref[pl.ds(2 * tile, 2), 0] = (
                (totals[1] / total).astype(jnp.bfloat16).reshape(2, rows, head_dim)
            )
        return carry

    lax.fori_loop(0, tiles // 2, step, 0)


def attend_kernel(band_ref, source_ref, *refs, scale):
    out_ref, *buffers, data_ref, done = refs[-7:]
    early = pltpu.make_async_copy(source_ref.at[:, :2], data_ref.at[:, :2], done.at[0])
    late = pltpu.make_async_copy(source_ref.at[:, 2:], data_ref.at[:, 2:], done.at[1])
    early.start()
    late.start()
    early.wait()
    stripe_len = data_ref.shape[0]
    band = band_ref[0]
    quarter = stripe_len // 4
    level = jnp.minimum(2 * band + 1, stripe_len - 1) // quarter
    for index in range(4):

        @pl.when((band >= 0) & (level == index))
        def _():
            attend_width(
                (index + 1) * quarter,
                band,
                data_ref,
                out_ref,
                buffers[:2],
                buffers[2:],
                scale,
                late,
            )

    @pl.when(band < 0)
    def _():
        late.wait()


def cross_kernel(query_ref, key_ref, value_ref, out_ref, *, head_dim, scale, group):
    def step(index, carry):
        for offset in range(group):
            head = index * group + offset
            columns = pl.ds(pl.multiple_of(head * head_dim, head_dim), head_dim)
            scores = lax.dot_general(
                query_ref[:, columns],
                key_ref[:, columns],
                (((1,), (1,)), ((), ())),
                preferred_element_type=jnp.float32,
            )
            peak = jnp.max(scores, axis=1, keepdims=True)
            weights = jnp.exp2((scores - peak) * (scale * LOG2_E))
            total = jnp.sum(weights, axis=1, keepdims=True)
            running = jnp.dot(
                weights.astype(jnp.bfloat16),
                value_ref[:, columns],
                preferred_element_type=jnp.float32,
            )
            out_ref[:, columns] = (running / total).astype(jnp.bfloat16)
        return carry

    lax.fori_loop(0, query_ref.shape[1] // head_dim // group, step, 0)


def pairs_kernel(*refs):
    for turn, own_ref in enumerate(refs[:-1]):
        refs[-1][turn] = own_ref[:, 1:]


def narrow_kernel(place_ref, *refs, scale):
    own_refs, (low_ref, high_ref) = refs[:SEATS], refs[SEATS : SEATS + 2]
    out_refs, (query_ref, key_ref, value_ref) = refs[SEATS + 2 : -3], refs[-3:]
    per_run, _, _, _ = own_refs[0].shape
    seat, first = place_ref[0], place_ref[1]

    def step(run, carry):
        band = place_ref[2 + run]
        for turn in range(SEATS):
            there = seat ^ turn
            query_ref[there] = own_refs[turn][run, 0]
            key_ref[SEATS + there] = own_refs[turn][run, 1]
            value_ref[SEATS + there] = own_refs[turn][run, 2]
            key_ref[there] = low_ref[turn, run, 0]
            value_ref[there] = low_ref[turn, run, 1]
            key_ref[2 * SEATS + there] = high_ref[turn, run, 0]
            value_ref[2 * SEATS + there] = high_ref[turn, run, 1]

        def attend(turn):
            there = seat ^ turn
            query = query_ref[there]
            tiles = []
            for gap in range(-REACH, REACH + 1):
                scores = lax.dot_general(
                    query,
                    key_ref[SEATS + there + gap],
                    (((1,), (1,)), ((), ())),
                    preferred_element_type=jnp.float32,
                )
                if gap:
                    block = first + there + gap
                    outside = (abs(gap) > band) | (block < 0) | (block >= SB)
                    scores = scores + jnp.where(outside, -jnp.inf, 0.0).astype(jnp.float32)
                tiles.append(scores)
            peak = jnp.max(functools.reduce(jnp.maximum, tiles), axis=1, keepdims=True)
            total, running = 0.0, 0.0
            for gap, scores in enumerate(tiles, -REACH):
                weights = jnp.exp2((scores - peak) * (scale * LOG2_E))
                total = total + weights
                running = running + jnp.dot(
                    weights.astype(jnp.bfloat16),
                    value_ref[SEATS + there + gap],
                    preferred_element_type=jnp.float32,
                )
            total = jnp.sum(total, axis=1, keepdims=True)
            out_refs[turn][run] = (running / total).astype(jnp.bfloat16)

        for turn in range(SEATS):
            attend(turn)
        return carry

    lax.fori_loop(0, per_run, step, 0)


def project_kernel(context_ref, key_ref, value_ref, out_ref, total_ref):
    weights = jnp.concatenate([key_ref[...], value_ref[...]], axis=0)
    product = lax.dot_general(
        context_ref[...], weights, (((1,), (1,)), ((), ())), preferred_element_type=jnp.float32
    )

    @pl.when(pl.program_id(0) == 0)
    def _():
        total_ref[...] = product

    @pl.when(pl.program_id(0) > 0)
    def _():
        total_ref[...] += product

    @pl.when(pl.program_id(0) == pl.num_programs(0) - 1)
    def _():
        out_ref[0] = total_ref[...].astype(jnp.bfloat16)


def project(context, key_weight, value_weight, steps=2):
    text_len, depth = context.shape
    columns = key_weight.shape[1]
    part = depth // steps
    weight_spec = pl.BlockSpec((columns, part), lambda step: (0, step))
    return pl.pallas_call(
        project_kernel,
        out_shape=jax.ShapeDtypeStruct((1, text_len, 2 * columns), jnp.bfloat16),
        grid=(steps,),
        in_specs=[
            pl.BlockSpec((text_len, part), lambda step: (0, step)),
            weight_spec,
            weight_spec,
        ],
        out_specs=pl.BlockSpec((1, text_len, 2 * columns), lambda step: (0, 0, 0)),
        scratch_shapes=[pltpu.VMEM((text_len, 2 * columns), jnp.float32)],
        name="project",
    )(context, key_weight.T, value_weight.T)


def split_kernel(place_ref, query_ref, out_ref):
    count, _, pair_width = out_ref.shape

    def fill(entry, carry):
        pair = 2 * entry + 1 - place_ref[1]
        columns = pl.ds(pl.multiple_of(pair * pair_width, pair_width), pair_width)
        out_ref[entry] = query_ref[:, columns]
        return carry

    lax.fori_loop(0, count, fill, 0)


def merge_kernel(place_ref, own_ref, came_ref, out_ref):
    count, _, pair_width = own_ref.shape

    def fill(entry, carry):
        for offset, part_ref in ((0, own_ref), (1, came_ref)):
            pair = 2 * entry + (place_ref[1] ^ offset)
            columns = pl.ds(pl.multiple_of(pair * pair_width, pair_width), pair_width)
            out_ref[:, columns] = part_ref[entry]
        return carry

    lax.fori_loop(0, count, fill, 0)


def cross_pairs_kernel(
    place_ref,
    query_ref,
    guest_ref,
    mine_ref,
    other_ref,
    own_ref,
    sent_ref,
    key_ref,
    value_ref,
    *,
    head_dim,
    scale,
):
    entries, _, pair_width = mine_ref.shape
    rows = query_ref.shape[0]
    columns = pair_width // 2
    bits = entries.bit_length() - 1

    def attend(even_ref, odd_ref):
        def step(entry, carry):
            plane = place_ref[0]
            for bit in range(bits):
                plane = plane ^ (((entry >> bit) & 1) << (bits - 1 - bit))
            key_ref[:, :columns] = even_ref[entry, :, :columns]
            key_ref[:, columns:] = odd_ref[entry, :, :columns]
            value_ref[:, :columns] = even_ref[entry, :, columns:]
            value_ref[:, columns:] = odd_ref[entry, :, columns:]
            first = (2 * plane + place_ref[1]) * pair_width
            for offset in range(pair_width // head_dim):
                source = pl.ds(offset * head_dim, head_dim)
                target = pl.ds(pl.multiple_of(first + offset * head_dim, head_dim), head_dim)
                query = jnp.concatenate(
                    [query_ref[:, target], guest_ref[plane, :, source]], axis=0
                )
                scores = lax.dot_general(
                    query,
                    key_ref[:, source],
                    (((1,), (1,)), ((), ())),
                    preferred_element_type=jnp.float32,
                )
                peak = jnp.max(scores, axis=1, keepdims=True)
                weights = jnp.exp2((scores - peak) * (scale * LOG2_E))
                total = jnp.sum(weights, axis=1, keepdims=True)
                running = jnp.dot(
                    weights.astype(jnp.bfloat16),
                    value_ref[:, source],
                    preferred_element_type=jnp.float32,
                )
                result = (running / total).astype(jnp.bfloat16)
                own_ref[plane, :, source] = result[:rows]
                sent_ref[plane, :, source] = result[rows:]
            return carry

        lax.fori_loop(0, entries, step, 0)

    @pl.when(place_ref[2] == 0)
    def _():
        attend(mine_ref, other_ref)

    @pl.when(place_ref[2] == 1)
    def _():
        attend(other_ref, mine_ref)


def swap(values, distance):
    devices = lax.axis_size("seq")
    return lax.ppermute(values, "seq", [(source, source ^ distance) for source in range(devices)])


def doubles(key_weight, head_dim):
    devices = lax.axis_size("seq")
    return (2 * key_weight.shape[1]) % head_dim == 0 and devices % 4 == 0 and devices & (devices - 1) == 0


def cross_attention(cross_query, context, key_weight, value_weight, head_dim, scale, text):
    devices = lax.axis_size("seq")
    device = lax.axis_index("seq")
    tok_rows, width = cross_query.shape
    out_shape = jax.ShapeDtypeStruct((tok_rows, width), jnp.bfloat16)
    vmem = pl.BlockSpec(memory_space=pltpu.VMEM)
    smem = pl.BlockSpec(memory_space=pltpu.SMEM)
    if text is None:
        text_key = jnp.dot(context, key_weight, preferred_element_type=jnp.float32)
        text_value = jnp.dot(context, value_weight, preferred_element_type=jnp.float32)
        return pl.pallas_call(
            functools.partial(cross_kernel, head_dim=head_dim, scale=scale, group=4),
            out_shape=out_shape,
            in_specs=[vmem, vmem, vmem],
            out_specs=vmem,
            name="cross",
            compiler_params=ROOM,
        )(
            cross_query,
            lax.all_gather(text_key.astype(jnp.bfloat16), "seq", axis=1, tiled=True),
            lax.all_gather(text_value.astype(jnp.bfloat16), "seq", axis=1, tiled=True),
        )
    place = jnp.stack([device // 4, device // 2 % 2, device % 2]).astype(jnp.int32)
    pair_shape = text.shape[1:]
    part_shape = jax.ShapeDtypeStruct((devices // 4, tok_rows, pair_shape[1]), jnp.bfloat16)
    leaving = pl.pallas_call(
        split_kernel,
        out_shape=part_shape,
        in_specs=[smem, vmem],
        out_specs=vmem,
        name="split",
        compiler_params=ROOM,
    )(place, cross_query)
    guests = swap(leaving, 2)
    distance = devices // 4
    while distance > 2:
        came = swap(text, distance)
        text = jnp.concatenate([text, came], axis=0)
        distance //= 2
    other = swap(text, 1)
    own, sent = pl.pallas_call(
        functools.partial(cross_pairs_kernel, head_dim=head_dim, scale=scale),
        out_shape=[part_shape] * 2,
        in_specs=[smem] + [vmem] * 4,
        out_specs=[vmem] * 2,
        scratch_shapes=[pltpu.VMEM(pair_shape, jnp.bfloat16)] * 2,
        name="cross",
        compiler_params=ROOM,
    )(place, cross_query, guests, text, other)
    back = swap(sent, 2)
    return pl.pallas_call(
        merge_kernel,
        out_shape=out_shape,
        in_specs=[smem, vmem, vmem],
        out_specs=vmem,
        name="merge",
        compiler_params=ROOM,
    )(place, own, back)


def exchange(values):
    devices = lax.axis_size("seq")
    return lax.all_to_all(
        values,
        "seq",
        split_axis=0,
        concat_axis=0,
        tiled=True,
        axis_index_groups=[list(range(first, first + SB)) for first in range(0, devices, SB)],
    )


def pack(order, sources, shapes, head_dim):
    vmem = pl.BlockSpec(memory_space=pltpu.VMEM)
    return pl.pallas_call(
        functools.partial(pack_kernel, head_dim=head_dim),
        out_shape=shapes,
        in_specs=[pl.BlockSpec(memory_space=pltpu.SMEM)] + [vmem] * 3,
        out_specs=[vmem] * len(shapes),
        name="pack",
    )(order, *sources)


def run_slots(outgoing, bands, scale):
    stripe_len, _, tok_rows, head_dim = outgoing[0].shape
    result = None
    for index, values in enumerate(outgoing):
        arrived = exchange(values)
        result = pl.pallas_call(
            functools.partial(attend_kernel, scale=scale),
            out_shape=jax.ShapeDtypeStruct(
                (stripe_len, len(outgoing), tok_rows, head_dim), jnp.bfloat16
            ),
            grid=(1,),
            in_specs=[
                pl.BlockSpec(memory_space=pltpu.SMEM),
                pl.BlockSpec(memory_space=pl.ANY),
            ]
            + ([] if result is None else [pl.BlockSpec(memory_space=pl.ANY)]),
            out_specs=pl.BlockSpec(
                (stripe_len, 1, tok_rows, head_dim),
                lambda step, index=index: (0, index, 0, 0),
            ),
            scratch_shapes=[
                pltpu.VMEM((2 * tok_rows, stripe_len * tok_rows), jnp.float32),
                pltpu.VMEM((2 * tok_rows, stripe_len * tok_rows), jnp.float32),
                pltpu.VMEM((2 * tok_rows, tok_rows), jnp.float32),
                pltpu.VMEM((2 * tok_rows, tok_rows), jnp.float32),
                pltpu.VMEM(values.shape, jnp.bfloat16),
                pltpu.SemaphoreType.DMA((2,)),
            ],
            input_output_aliases={} if result is None else {2: 0},
            compiler_params=ROOM,
            name="attend",
        )(bands[index : index + 1], arrived, *([] if result is None else [result]))
    return exchange(result)


def seat_rank(place):
    return jnp.where(place < SB // 2, 2 * place, 2 * (SB - 1 - place) + 1)


def layer(
    self_query, self_key, self_value, cross_query, context, key_weight, value_weight, band_width
):
    devices = lax.axis_size("seq")
    device = lax.axis_index("seq")
    tok_rows, width = self_query.shape
    head_count = band_width.shape[0]
    head_dim = width // head_count
    scale = 1.0 / math.sqrt(head_dim)
    vmem = pl.BlockSpec(memory_space=pltpu.VMEM)
    smem = pl.BlockSpec(memory_space=pltpu.SMEM)
    seat, turn_seat = device % SEATS, device % SB
    sources = (self_query, self_key, self_value)

    def block_array(*lead):
        return jax.ShapeDtypeStruct(lead + (tok_rows, head_dim), jnp.bfloat16)

    text = None
    if doubles(key_weight, head_dim):
        text = project(context, key_weight, value_weight)
        came = swap(text, devices // 2)
        text = jnp.concatenate([text, came], axis=0)

    whole_run = head_count // SB
    rest = head_count - whole_run * SB
    narrow_run = (rest + SEATS - 1) // SEATS
    head_ids = jnp.arange(head_count, dtype=jnp.int32)
    ahead = (band_width[None, :] > band_width[:, None]) | (
        (band_width[None, :] == band_width[:, None]) & (head_ids[None, :] < head_ids[:, None])
    )
    rank = jnp.sum(ahead.astype(jnp.int32), axis=1)
    close = jnp.sum((band_width <= REACH).astype(jnp.int32)) >= rest
    slot_ids = jnp.arange(SB * (whole_run + 1), dtype=jnp.int32)
    run, place = slot_ids // SB, slot_ids % SB
    wanted = run * SB + seat_rank(place)
    runs = jnp.arange(whole_run + 1, dtype=jnp.int32)
    mine = runs * SB + seat_rank(turn_seat)
    slot_ids = jnp.arange(SEATS * narrow_run, dtype=jnp.int32)
    run, place = slot_ids % narrow_run, (slot_ids // narrow_run) ^ seat
    near = SB * whole_run + run * SEATS + jnp.where(run % 2 == 0, place, SEATS - 1 - place)
    wanted = jnp.concatenate([wanted, near])
    mine = jnp.concatenate([mine, near[:narrow_run]])
    order = jnp.sum(jnp.where(wanted[:, None] == rank[None, :], head_ids + 1, 0), axis=1) - 1
    bands = jnp.sum(jnp.where(mine[:, None] == rank[None, :], band_width + 1, 0), axis=1) - 1
    wide_slots, last_slots = SB * whole_run, SB * (whole_run + 1)

    shapes = [block_array(SB, 3)] * whole_run + [block_array(narrow_run, 3)] * SEATS
    packed = pack(
        jnp.concatenate([order[:wide_slots], order[last_slots:]]), sources, shapes, head_dim
    )
    returned = run_slots(packed[:whole_run], bands[:whole_run], scale)
    own = [packed[whole_run]]
    for turn in range(1, SEATS):
        own.append(swap(packed[whole_run + turn], turn))
    pairs = pl.pallas_call(
        pairs_kernel,
        out_shape=block_array(SEATS, narrow_run, 2),
        in_specs=[vmem] * SEATS,
        out_specs=vmem,
        name="pairs",
    )(*own)
    upward = [
        (source, source + SEATS)
        for source in range(devices - SEATS)
        if source // SB == (source + SEATS) // SB
    ]
    low = lax.ppermute(pairs, "seq", upward)
    high = lax.ppermute(pairs, "seq", [(high, low) for low, high in upward])
    places = jnp.stack([seat, turn_seat - seat]).astype(jnp.int32)
    near_out = pl.pallas_call(
        functools.partial(narrow_kernel, scale=scale),
        out_shape=[block_array(narrow_run)] * SEATS,
        in_specs=[smem] + [vmem] * (SEATS + 2),
        out_specs=[vmem] * SEATS,
        scratch_shapes=[
            pltpu.VMEM((count * SEATS, tok_rows, head_dim), jnp.bfloat16)
            for count in (1, 3, 3)
        ],
        name="narrow",
        compiler_params=ROOM,
    )(jnp.concatenate([places, bands[whole_run + 1 :]]), *own, low, high)
    nears = [near_out[0]]
    for turn in range(1, SEATS):
        nears.append(swap(near_out[turn], turn))
    cross_out = cross_attention(
        cross_query, context, key_weight, value_weight, head_dim, scale, text
    )

    def full(sources):
        (outgoing,) = pack(
            order[wide_slots:last_slots], sources, [block_array(SB, 3)], head_dim
        )
        return run_slots([outgoing], bands[whole_run : whole_run + 1], scale)

    def short(sources):
        return jnp.zeros((SB, 1, tok_rows, head_dim), jnp.bfloat16)

    last = lax.cond(close, short, full, sources)
    slot_ids = jnp.arange(order.shape[0], dtype=jnp.int32)
    from_last = (slot_ids >= wide_slots) & (slot_ids < last_slots)
    unused = jnp.where(close, from_last, slot_ids >= last_slots)
    parts = [returned, last] + [part[:, None] for part in nears]
    self_out = pl.pallas_call(
        functools.partial(unpack_kernel, head_dim=head_dim),
        out_shape=jax.ShapeDtypeStruct((tok_rows, width), jnp.bfloat16),
        in_specs=[smem] + [vmem] * len(parts),
        out_specs=pl.BlockSpec(memory_space=pl.ANY),
        scratch_shapes=[pltpu.SemaphoreType.DMA],
        name="unpack",
        compiler_params=ROOM,
    )(jnp.where(unused, -1, order), *parts)
    return (self_out, cross_out)


def solution(mesh):
    in_specs = (
        P(("groups", "seq"), None),
        P(("groups", "seq"), None),
        P(("groups", "seq"), None),
        P(("groups", "seq"), None),
        P("groups", None),
        P(None, "seq"),
        P(None, "seq"),
        P(),
    )
    out_specs = (P(("groups", "seq"), None), P(("groups", "seq"), None))
    return jax.shard_map(layer, mesh=mesh, in_specs=in_specs, out_specs=out_specs, check_vma=False)
```

```python
import functools
import math

import jax
import jax.numpy as jnp
from jax import lax
from jax.experimental import pallas as pl
from jax.experimental.pallas import tpu as pltpu
from jax.sharding import PartitionSpec as P


SB = 16
SEATS = 4
REACH = 4
ROOM = pltpu.CompilerParams(vmem_limit_bytes=24 << 20)
LOG2_E = 1.4426950408889634


def pack_kernel(order_ref, query_ref, key_ref, value_ref, *out_refs, head_dim):
    sources = (query_ref, key_ref, value_ref)
    first = 0
    for out_ref in out_refs:
        seats, _ = out_ref.shape[:2]

        def fill(seat, carry, out_ref=out_ref, first=first):
            head = jnp.maximum(order_ref[first + seat], 0)
            columns = pl.ds(pl.multiple_of(head * head_dim, head_dim), head_dim)
            for index, source in enumerate(sources):
                out_ref[seat, index] = source[:, columns]
            return carry

        lax.fori_loop(0, seats, fill, 0)
        first += seats


def unpack_kernel(order_ref, *refs, head_dim):
    out_ref, done = refs[-2:]
    first = 0
    for returned_ref in refs[:-2]:
        seats, runs = returned_ref.shape[:2]
        for run in range(runs):

            def fill(seat, carry, returned_ref=returned_ref, first=first, run=run):
                head = order_ref[first + seat]

                @pl.when(head >= 0)
                def _():
                    columns = pl.ds(pl.multiple_of(head * head_dim, head_dim), head_dim)
                    pltpu.make_async_copy(
                        returned_ref.at[seat, run], out_ref.at[:, columns], done
                    ).start()

                return carry

            lax.fori_loop(0, seats, fill, 0)
            first += seats
    pltpu.make_async_copy(out_ref, out_ref, done).wait()


def score_step(tile, chunk, width, band, data_ref, score_ref, peak):
    stripe_len, _, rows, head_dim = data_ref.shape
    start = jnp.clip(2 * tile - band, 0, stripe_len - width)
    query = data_ref[pl.ds(2 * tile, 2), 0].reshape(2 * rows, head_dim)
    keys = data_ref[pl.ds(start + chunk, 2), 1].reshape(2 * rows, head_dim)
    scores = lax.dot_general(
        query, keys, (((1,), (1,)), ((), ())), preferred_element_type=jnp.float32
    )
    for part in range(2):
        key_block = start + chunk + part
        halves = []
        for half in range(2):
            outside = jnp.abs(2 * tile + half - key_block) > band
            bias = jnp.where(outside, -jnp.inf, 0.0).astype(jnp.float32)
            halves.append(
                scores[half * rows : (half + 1) * rows, part * rows : (part + 1) * rows] + bias
            )
        masked = jnp.concatenate(halves, axis=0)
        score_ref[:, (chunk + part) * rows : (chunk + part + 1) * rows] = masked
        peak = masked if peak is None else jnp.maximum(peak, masked)
    return peak


def value_step(tile, chunk, width, band, data_ref, score_ref, peak, totals, scale):
    stripe_len, _, rows, head_dim = data_ref.shape
    start = jnp.clip(2 * tile - band, 0, stripe_len - width)
    weights = jnp.exp2(
        (score_ref[:, chunk * rows : (chunk + 2) * rows] - peak) * (scale * LOG2_E)
    )
    values = data_ref[pl.ds(start + chunk, 2), 2].reshape(2 * rows, head_dim)
    partial = weights[:, :rows] + weights[:, rows:]
    product = jnp.dot(weights.astype(jnp.bfloat16), values, preferred_element_type=jnp.float32)
    if totals is None:
        return partial, product
    return totals[0] + partial, totals[1] + product


def attend_width(width, band, data_ref, out_ref, score_refs, peak_refs, scale, late):
    stripe_len, _, rows, head_dim = data_ref.shape
    tiles = stripe_len // 2
    peak = None
    for chunk in range(0, width, 2):
        peak = score_step(0, chunk, width, band, data_ref, score_refs[0], peak)
    peak_refs[0][...] = peak
    late.wait()

    def step(pair, carry):
        for turn in range(2):
            tile = 2 * pair + turn
            following = jnp.minimum(tile + 1, tiles - 1)
            peak = jnp.max(peak_refs[turn][...], axis=1, keepdims=True)
            ahead, totals = None, None
            for chunk in range(0, width, 2):
                ahead = score_step(
                    following, chunk, width, band, data_ref, score_refs[1 - turn], ahead
                )
                totals = value_step(
                    tile, chunk, width, band, data_ref, score_refs[turn], peak, totals, scale
                )
            peak_refs[1 - turn][...] = ahead
            total = jnp.sum(totals[0], axis=1, keepdims=True)
            out_ref[pl.ds(2 * tile, 2), 0] = (
                (totals[1] / total).astype(jnp.bfloat16).reshape(2, rows, head_dim)
            )
        return carry

    lax.fori_loop(0, tiles // 2, step, 0)


def attend_kernel(band_ref, source_ref, *refs, scale):
    out_ref, *buffers, data_ref, done = refs[-7:]
    early = pltpu.make_async_copy(source_ref.at[:, :2], data_ref.at[:, :2], done.at[0])
    late = pltpu.make_async_copy(source_ref.at[:, 2:], data_ref.at[:, 2:], done.at[1])
    early.start()
    late.start()
    early.wait()
    stripe_len = data_ref.shape[0]
    band = band_ref[0]
    reach = jnp.minimum(2 * band + 2, stripe_len)
    widths = (stripe_len // 2, stripe_len * 5 // 8, stripe_len * 3 // 4, stripe_len)
    for below, width in zip((0,) + widths[:-1], widths):

        @pl.when((band >= 0) & (reach > below) & (reach <= width))
        def _():
            attend_width(
                width,
                band,
                data_ref,
                out_ref,
                buffers[:2],
                buffers[2:],
                scale,
                late,
            )

    @pl.when(band < 0)
    def _():
        late.wait()


def cross_kernel(query_ref, key_ref, value_ref, out_ref, *, head_dim, scale, group):
    def step(index, carry):
        for offset in range(group):
            head = index * group + offset
            columns = pl.ds(pl.multiple_of(head * head_dim, head_dim), head_dim)
            scores = lax.dot_general(
                query_ref[:, columns],
                key_ref[:, columns],
                (((1,), (1,)), ((), ())),
                preferred_element_type=jnp.float32,
            )
            peak = jnp.max(scores, axis=1, keepdims=True)
            weights = jnp.exp2((scores - peak) * (scale * LOG2_E))
            total = jnp.sum(weights, axis=1, keepdims=True)
            running = jnp.dot(
                weights.astype(jnp.bfloat16),
                value_ref[:, columns],
                preferred_element_type=jnp.float32,
            )
            out_ref[:, columns] = (running / total).astype(jnp.bfloat16)
        return carry

    lax.fori_loop(0, query_ref.shape[1] // head_dim // group, step, 0)


def pairs_kernel(*refs):
    for turn, own_ref in enumerate(refs[:-1]):
        refs[-1][turn] = own_ref[:, 1:]


def narrow_kernel(place_ref, *refs, scale):
    own_refs, (low_ref, high_ref) = refs[:SEATS], refs[SEATS : SEATS + 2]
    out_refs, (query_ref, key_ref, value_ref) = refs[SEATS + 2 : -3], refs[-3:]
    per_run, _, _, _ = own_refs[0].shape
    seat, first = place_ref[0], place_ref[1]

    def step(run, carry):
        band = place_ref[2 + run]
        for turn in range(SEATS):
            there = seat ^ turn
            query_ref[there] = own_refs[turn][run, 0]
            key_ref[SEATS + there] = own_refs[turn][run, 1]
            value_ref[SEATS + there] = own_refs[turn][run, 2]
            key_ref[there] = low_ref[turn, run, 0]
            value_ref[there] = low_ref[turn, run, 1]
            key_ref[2 * SEATS + there] = high_ref[turn, run, 0]
            value_ref[2 * SEATS + there] = high_ref[turn, run, 1]

        def attend(turn):
            there = seat ^ turn
            query = query_ref[there]
            tiles = []
            for gap in range(-REACH, REACH + 1):
                scores = lax.dot_general(
                    query,
                    key_ref[SEATS + there + gap],
                    (((1,), (1,)), ((), ())),
                    preferred_element_type=jnp.float32,
                )
                if gap:
                    block = first + there + gap
                    outside = (abs(gap) > band) | (block < 0) | (block >= SB)
                    scores = scores + jnp.where(outside, -jnp.inf, 0.0).astype(jnp.float32)
                tiles.append(scores)
            peak = jnp.max(functools.reduce(jnp.maximum, tiles), axis=1, keepdims=True)
            total, running = 0.0, 0.0
            for gap, scores in enumerate(tiles, -REACH):
                weights = jnp.exp2((scores - peak) * (scale * LOG2_E))
                total = total + weights
                running = running + jnp.dot(
                    weights.astype(jnp.bfloat16),
                    value_ref[SEATS + there + gap],
                    preferred_element_type=jnp.float32,
                )
            total = jnp.sum(total, axis=1, keepdims=True)
            out_refs[turn][run] = (running / total).astype(jnp.bfloat16)

        for turn in range(SEATS):
            attend(turn)
        return carry

    lax.fori_loop(0, per_run, step, 0)


def project_kernel(context_ref, key_ref, value_ref, out_ref, total_ref):
    weights = jnp.concatenate([key_ref[...], value_ref[...]], axis=0)
    product = lax.dot_general(
        context_ref[...], weights, (((1,), (1,)), ((), ())), preferred_element_type=jnp.float32
    )

    @pl.when(pl.program_id(0) == 0)
    def _():
        total_ref[...] = product

    @pl.when(pl.program_id(0) > 0)
    def _():
        total_ref[...] += product

    @pl.when(pl.program_id(0) == pl.num_programs(0) - 1)
    def _():
        out_ref[0] = total_ref[...].astype(jnp.bfloat16)


def project(context, key_weight, value_weight, steps=2):
    text_len, depth = context.shape
    columns = key_weight.shape[1]
    part = depth // steps
    weight_spec = pl.BlockSpec((columns, part), lambda step: (0, step))
    return pl.pallas_call(
        project_kernel,
        out_shape=jax.ShapeDtypeStruct((1, text_len, 2 * columns), jnp.bfloat16),
        grid=(steps,),
        in_specs=[
            pl.BlockSpec((text_len, part), lambda step: (0, step)),
            weight_spec,
            weight_spec,
        ],
        out_specs=pl.BlockSpec((1, text_len, 2 * columns), lambda step: (0, 0, 0)),
        scratch_shapes=[pltpu.VMEM((text_len, 2 * columns), jnp.float32)],
        name="project",
    )(context, key_weight.T, value_weight.T)


def split_kernel(place_ref, query_ref, out_ref):
    count, _, pair_width = out_ref.shape

    def fill(entry, carry):
        pair = 2 * entry + 1 - place_ref[1]
        columns = pl.ds(pl.multiple_of(pair * pair_width, pair_width), pair_width)
        out_ref[entry] = query_ref[:, columns]
        return carry

    lax.fori_loop(0, count, fill, 0)


def merge_kernel(place_ref, own_ref, came_ref, out_ref):
    count, _, pair_width = own_ref.shape

    def fill(entry, carry):
        for offset, part_ref in ((0, own_ref), (1, came_ref)):
            pair = 2 * entry + (place_ref[1] ^ offset)
            columns = pl.ds(pl.multiple_of(pair * pair_width, pair_width), pair_width)
            out_ref[:, columns] = part_ref[entry]
        return carry

    lax.fori_loop(0, count, fill, 0)


def cross_pairs_kernel(
    place_ref,
    query_ref,
    guest_ref,
    mine_ref,
    other_ref,
    own_ref,
    sent_ref,
    key_ref,
    value_ref,
    *,
    head_dim,
    scale,
):
    entries, _, pair_width = mine_ref.shape
    rows = query_ref.shape[0]
    columns = pair_width // 2
    bits = entries.bit_length() - 1

    def attend(even_ref, odd_ref):
        def step(entry, carry):
            plane = place_ref[0]
            for bit in range(bits):
                plane = plane ^ (((entry >> bit) & 1) << (bits - 1 - bit))
            key_ref[:, :columns] = even_ref[entry, :, :columns]
            key_ref[:, columns:] = odd_ref[entry, :, :columns]
            value_ref[:, :columns] = even_ref[entry, :, columns:]
            value_ref[:, columns:] = odd_ref[entry, :, columns:]
            first = (2 * plane + place_ref[1]) * pair_width
            for offset in range(pair_width // head_dim):
                source = pl.ds(offset * head_dim, head_dim)
                target = pl.ds(pl.multiple_of(first + offset * head_dim, head_dim), head_dim)
                query = jnp.concatenate(
                    [query_ref[:, target], guest_ref[plane, :, source]], axis=0
                )
                scores = lax.dot_general(
                    query,
                    key_ref[:, source],
                    (((1,), (1,)), ((), ())),
                    preferred_element_type=jnp.float32,
                )
                peak = jnp.max(scores, axis=1, keepdims=True)
                weights = jnp.exp2((scores - peak) * (scale * LOG2_E))
                total = jnp.sum(weights, axis=1, keepdims=True)
                running = jnp.dot(
                    weights.astype(jnp.bfloat16),
                    value_ref[:, source],
                    preferred_element_type=jnp.float32,
                )
                result = (running / total).astype(jnp.bfloat16)
                own_ref[plane, :, source] = result[:rows]
                sent_ref[plane, :, source] = result[rows:]
            return carry

        lax.fori_loop(0, entries, step, 0)

    @pl.when(place_ref[2] == 0)
    def _():
        attend(mine_ref, other_ref)

    @pl.when(place_ref[2] == 1)
    def _():
        attend(other_ref, mine_ref)


def swap(values, distance):
    devices = lax.axis_size("seq")
    return lax.ppermute(values, "seq", [(source, source ^ distance) for source in range(devices)])


def doubles(key_weight, head_dim):
    devices = lax.axis_size("seq")
    return (2 * key_weight.shape[1]) % head_dim == 0 and devices % 4 == 0 and devices & (devices - 1) == 0


def cross_attention(cross_query, context, key_weight, value_weight, head_dim, scale, text):
    devices = lax.axis_size("seq")
    device = lax.axis_index("seq")
    tok_rows, width = cross_query.shape
    out_shape = jax.ShapeDtypeStruct((tok_rows, width), jnp.bfloat16)
    vmem = pl.BlockSpec(memory_space=pltpu.VMEM)
    smem = pl.BlockSpec(memory_space=pltpu.SMEM)
    if text is None:
        text_key = jnp.dot(context, key_weight, preferred_element_type=jnp.float32)
        text_value = jnp.dot(context, value_weight, preferred_element_type=jnp.float32)
        return pl.pallas_call(
            functools.partial(cross_kernel, head_dim=head_dim, scale=scale, group=4),
            out_shape=out_shape,
            in_specs=[vmem, vmem, vmem],
            out_specs=vmem,
            name="cross",
            compiler_params=ROOM,
        )(
            cross_query,
            lax.all_gather(text_key.astype(jnp.bfloat16), "seq", axis=1, tiled=True),
            lax.all_gather(text_value.astype(jnp.bfloat16), "seq", axis=1, tiled=True),
        )
    place = jnp.stack([device // 4, device // 2 % 2, device % 2]).astype(jnp.int32)
    pair_shape = text.shape[1:]
    part_shape = jax.ShapeDtypeStruct((devices // 4, tok_rows, pair_shape[1]), jnp.bfloat16)
    leaving = pl.pallas_call(
        split_kernel,
        out_shape=part_shape,
        in_specs=[smem, vmem],
        out_specs=vmem,
        name="split",
        compiler_params=ROOM,
    )(place, cross_query)
    guests = swap(leaving, 2)
    distance = devices // 4
    while distance > 2:
        came = swap(text, distance)
        text = jnp.concatenate([text, came], axis=0)
        distance //= 2
    other = swap(text, 1)
    own, sent = pl.pallas_call(
        functools.partial(cross_pairs_kernel, head_dim=head_dim, scale=scale),
        out_shape=[part_shape] * 2,
        in_specs=[smem] + [vmem] * 4,
        out_specs=[vmem] * 2,
        scratch_shapes=[pltpu.VMEM(pair_shape, jnp.bfloat16)] * 2,
        name="cross",
        compiler_params=ROOM,
    )(place, cross_query, guests, text, other)
    back = swap(sent, 2)
    return pl.pallas_call(
        merge_kernel,
        out_shape=out_shape,
        in_specs=[smem, vmem, vmem],
        out_specs=vmem,
        name="merge",
        compiler_params=ROOM,
    )(place, own, back)


def exchange(values):
    devices = lax.axis_size("seq")
    return lax.all_to_all(
        values,
        "seq",
        split_axis=0,
        concat_axis=0,
        tiled=True,
        axis_index_groups=[list(range(first, first + SB)) for first in range(0, devices, SB)],
    )


def pack(order, sources, shapes, head_dim):
    vmem = pl.BlockSpec(memory_space=pltpu.VMEM)
    return pl.pallas_call(
        functools.partial(pack_kernel, head_dim=head_dim),
        out_shape=shapes,
        in_specs=[pl.BlockSpec(memory_space=pltpu.SMEM)] + [vmem] * 3,
        out_specs=[vmem] * len(shapes),
        name="pack",
    )(order, *sources)


def run_slots(outgoing, bands, scale):
    stripe_len, _, tok_rows, head_dim = outgoing[0].shape
    result = None
    for index, values in enumerate(outgoing):
        arrived = exchange(values)
        result = pl.pallas_call(
            functools.partial(attend_kernel, scale=scale),
            out_shape=jax.ShapeDtypeStruct(
                (stripe_len, len(outgoing), tok_rows, head_dim), jnp.bfloat16
            ),
            grid=(1,),
            in_specs=[
                pl.BlockSpec(memory_space=pltpu.SMEM),
                pl.BlockSpec(memory_space=pl.ANY),
            ]
            + ([] if result is None else [pl.BlockSpec(memory_space=pl.ANY)]),
            out_specs=pl.BlockSpec(
                (stripe_len, 1, tok_rows, head_dim),
                lambda step, index=index: (0, index, 0, 0),
            ),
            scratch_shapes=[
                pltpu.VMEM((2 * tok_rows, stripe_len * tok_rows), jnp.float32),
                pltpu.VMEM((2 * tok_rows, stripe_len * tok_rows), jnp.float32),
                pltpu.VMEM((2 * tok_rows, tok_rows), jnp.float32),
                pltpu.VMEM((2 * tok_rows, tok_rows), jnp.float32),
                pltpu.VMEM(values.shape, jnp.bfloat16),
                pltpu.SemaphoreType.DMA((2,)),
            ],
            input_output_aliases={} if result is None else {2: 0},
            compiler_params=pltpu.CompilerParams(vmem_limit_bytes=40 << 20),
            name="attend",
        )(bands[index : index + 1], arrived, *([] if result is None else [result]))
    return exchange(result)


def seat_rank(place):
    return jnp.where(place < SB // 2, 2 * place, 2 * (SB - 1 - place) + 1)


def layer(
    self_query, self_key, self_value, cross_query, context, key_weight, value_weight, band_width
):
    devices = lax.axis_size("seq")
    device = lax.axis_index("seq")
    tok_rows, width = self_query.shape
    head_count = band_width.shape[0]
    head_dim = width // head_count
    scale = 1.0 / math.sqrt(head_dim)
    vmem = pl.BlockSpec(memory_space=pltpu.VMEM)
    smem = pl.BlockSpec(memory_space=pltpu.SMEM)
    seat, turn_seat = device % SEATS, device % SB
    sources = (self_query, self_key, self_value)

    def block_array(*lead):
        return jax.ShapeDtypeStruct(lead + (tok_rows, head_dim), jnp.bfloat16)

    text = None
    if doubles(key_weight, head_dim):
        text = project(context, key_weight, value_weight)
        came = swap(text, devices // 2)
        text = jnp.concatenate([text, came], axis=0)

    whole_run = head_count // SB
    rest = head_count - whole_run * SB
    narrow_run = (rest + SEATS - 1) // SEATS
    head_ids = jnp.arange(head_count, dtype=jnp.int32)
    ahead = (band_width[None, :] > band_width[:, None]) | (
        (band_width[None, :] == band_width[:, None]) & (head_ids[None, :] < head_ids[:, None])
    )
    rank = jnp.sum(ahead.astype(jnp.int32), axis=1)
    close = jnp.sum((band_width <= REACH).astype(jnp.int32)) >= rest
    slot_ids = jnp.arange(SB * (whole_run + 1), dtype=jnp.int32)
    run, place = slot_ids // SB, slot_ids % SB
    wanted = run * SB + seat_rank(place)
    runs = jnp.arange(whole_run + 1, dtype=jnp.int32)
    mine = runs * SB + seat_rank(turn_seat)
    slot_ids = jnp.arange(SEATS * narrow_run, dtype=jnp.int32)
    run, place = slot_ids % narrow_run, (slot_ids // narrow_run) ^ seat
    near = SB * whole_run + run * SEATS + jnp.where(run % 2 == 0, place, SEATS - 1 - place)
    wanted = jnp.concatenate([wanted, near])
    mine = jnp.concatenate([mine, near[:narrow_run]])
    order = jnp.sum(jnp.where(wanted[:, None] == rank[None, :], head_ids + 1, 0), axis=1) - 1
    bands = jnp.sum(jnp.where(mine[:, None] == rank[None, :], band_width + 1, 0), axis=1) - 1
    wide_slots, last_slots = SB * whole_run, SB * (whole_run + 1)

    shapes = [block_array(SB, 3)] * whole_run + [block_array(narrow_run, 3)] * SEATS
    packed = pack(
        jnp.concatenate([order[:wide_slots], order[last_slots:]]), sources, shapes, head_dim
    )
    returned = run_slots(packed[:whole_run], bands[:whole_run], scale)
    own = [packed[whole_run]]
    for turn in range(1, SEATS):
        own.append(swap(packed[whole_run + turn], turn))
    pairs = pl.pallas_call(
        pairs_kernel,
        out_shape=block_array(SEATS, narrow_run, 2),
        in_specs=[vmem] * SEATS,
        out_specs=vmem,
        name="pairs",
    )(*own)
    upward = [
        (source, source + SEATS)
        for source in range(devices - SEATS)
        if source // SB == (source + SEATS) // SB
    ]
    low = lax.ppermute(pairs, "seq", upward)
    high = lax.ppermute(pairs, "seq", [(high, low) for low, high in upward])
    places = jnp.stack([seat, turn_seat - seat]).astype(jnp.int32)
    near_out = pl.pallas_call(
        functools.partial(narrow_kernel, scale=scale),
        out_shape=[block_array(narrow_run)] * SEATS,
        in_specs=[smem] + [vmem] * (SEATS + 2),
        out_specs=[vmem] * SEATS,
        scratch_shapes=[
            pltpu.VMEM((count * SEATS, tok_rows, head_dim), jnp.bfloat16)
            for count in (1, 3, 3)
        ],
        name="narrow",
        compiler_params=ROOM,
    )(jnp.concatenate([places, bands[whole_run + 1 :]]), *own, low, high)
    nears = [near_out[0]]
    for turn in range(1, SEATS):
        nears.append(swap(near_out[turn], turn))
    cross_out = cross_attention(
        cross_query, context, key_weight, value_weight, head_dim, scale, text
    )

    def full(sources):
        (outgoing,) = pack(
            order[wide_slots:last_slots], sources, [block_array(SB, 3)], head_dim
        )
        return run_slots([outgoing], bands[whole_run : whole_run + 1], scale)

    def short(sources):
        return jnp.zeros((SB, 1, tok_rows, head_dim), jnp.bfloat16)

    last = lax.cond(close, short, full, sources)
    slot_ids = jnp.arange(order.shape[0], dtype=jnp.int32)
    from_last = (slot_ids >= wide_slots) & (slot_ids < last_slots)
    unused = jnp.where(close, from_last, slot_ids >= last_slots)
    parts = [returned, last] + [part[:, None] for part in nears]
    self_out = pl.pallas_call(
        functools.partial(unpack_kernel, head_dim=head_dim),
        out_shape=jax.ShapeDtypeStruct((tok_rows, width), jnp.bfloat16),
        in_specs=[smem] + [vmem] * len(parts),
        out_specs=pl.BlockSpec(memory_space=pl.ANY),
        scratch_shapes=[pltpu.SemaphoreType.DMA],
        name="unpack",
        compiler_params=ROOM,
    )(jnp.where(unused, -1, order), *parts)
    return (self_out, cross_out)


def solution(mesh):
    in_specs = (
        P(("groups", "seq"), None),
        P(("groups", "seq"), None),
        P(("groups", "seq"), None),
        P(("groups", "seq"), None),
        P("groups", None),
        P(None, "seq"),
        P(None, "seq"),
        P(),
    )
    out_specs = (P(("groups", "seq"), None), P(("groups", "seq"), None))
    return jax.shard_map(layer, mesh=mesh, in_specs=in_specs, out_specs=out_specs, check_vma=False)
```
